1024 devices in a mesh: tm: 64 (over x_hi, z, core), space: 16 (over x_lo, y).
Axes of the slice: x: 4 (x_hi: 2, x_lo: 2; x = x_hi * 2 + x_lo), y: 8, z: 16, core: 2. Of those that a mesh axis runs over, the one named last changes fastest.
Arguments:
- y_first: bfloat16 [2, 64, 1024, 1024], P(None, 'tm', 'space'), may hold values from -6 to 6
- y_second: bfloat16 [2, 64, 1024, 1024], P(None, 'tm', 'space'), may hold values from -6 to 6
- grad_first: bfloat16 [2, 64, 1024, 1024], P(None, 'tm', 'space'), may hold values from -6 to 6
- grad_second: bfloat16 [2, 64, 1024, 1024], P(None, 'tm', 'space'), may hold values from -6 to 6
- pattern: int32 [64, 8], P('tm'), may hold values from 0 to 7, as said below
- time_qkv: bfloat16 [1024, 1536], replicated, may hold values from -3 to 3
- time_out: bfloat16 [512, 1024], replicated, may hold values from -0.25 to 0.25
- space_qkv: bfloat16 [1024, 1536], replicated, may hold values from -3 to 3
- space_out: bfloat16 [512, 1024], replicated, may hold values from -0.25 to 0.25
Outputs:
- x_first: bfloat16 [2, 64, 1024, 1024], P(None, 'tm', 'space')
- x_second: bfloat16 [2, 64, 1024, 1024], P(None, 'tm', 'space')
- dx_first: bfloat16 [2, 64, 1024, 1024], P(None, 'tm', 'space')
- dx_second: bfloat16 [2, 64, 1024, 1024], P(None, 'tm', 'space')
The draws below stay inside these ranges and needn't reach their ends.
Inputs may be any that keep to these rules, and one draw needn't show every extreme that they name: pattern[f, b] is b - 1, b or b + 1.
All inputs are finite; a program needn't handle non-finite values.
Results may differ from the reference program's by a relative error of at most 0.01.
Values may be sent and summed in bfloat16 or wider, within the bound.
No kernel may reach another device: no remote copies, remote signals or barrier semaphores. Data moves between devices by JAX's collectives and lax.ppermute only.
A program may use at most 64 MiB of HBM per device.

```python
import math
import jax
import jax.numpy as jnp
from jax import lax

D = 1024
HEADS = 8
HEAD_DIM = 64
INNER = 512
CLIPS = 2
P_DEV = 64
FRAMES = 64
PATCHES = 1024
NBLK = 8


def qkv_matrix(key, salt):
    local = jax.random.fold_in(key, salt)
    inner_w = HEADS * HEAD_DIM
    base = jnp.clip(jax.random.normal(local, (D, 3 * inner_w), jnp.float32), -4.0, 4.0) / math.sqrt(D)
    return base.astype(jnp.bfloat16)


def draw_time_qkv(key, part):
    return qkv_matrix(key, 11)


def draw_space_qkv(key, part):
    return qkv_matrix(key, 12)


def draw_pattern(key, part):
    step_by = jax.random.randint(jax.random.fold_in(key, 13), (FRAMES, NBLK), -1, 2, jnp.int32)
    blocks = jnp.arange(NBLK, dtype=jnp.int32)[None, :]
    beside = jnp.clip(blocks + step_by, 0, NBLK - 1)
    return beside.astype(jnp.int32)


def levels(stream_key, shape, pieces, smallest, high):
    def one(position, blocks):
        heights = jax.random.uniform(jax.random.fold_in(jax.random.fold_in(stream_key, 6), position), (blocks,), jnp.float32, smallest / len(pieces), high / len(pieces))
        return jnp.repeat(jnp.exp(heights), shape[position] // blocks).reshape((-1,) + (1,) * (len(shape) - position - 1))

    factor_of = one(*pieces[0])
    for cut in pieces[1:]:
        factor_of = factor_of * one(*cut)
    return factor_of


def scatter_about(own_key, shape, deviation, bound, cuts=(), held_as=jnp.bfloat16):
    entries = deviation * jax.random.normal(own_key, shape, jnp.float32)
    if cuts:
        entries = entries * levels(own_key, shape, cuts, -0.22, 0.18)
    return jnp.clip(entries, -bound, bound).astype(held_as)


def setup_inputs(seed: int = 0) -> dict:
    splits = jax.random.split(jax.random.key(seed), 10)
    return {
        "y_first": scatter_about(splits[0], (CLIPS, FRAMES, PATCHES, D), 1.0, 6.0, ((1, 64), (2, 16))),
        "y_second": scatter_about(splits[1], (CLIPS, FRAMES, PATCHES, D), 1.0, 6.0, ((1, 64), (2, 16))),
        "grad_first": scatter_about(splits[2], (CLIPS, FRAMES, PATCHES, D), 1.0, 6.0, ((1, 64), (2, 16))),
        "grad_second": scatter_about(splits[3], (CLIPS, FRAMES, PATCHES, D), 1.0, 6.0, ((1, 64), (2, 16))),
        "pattern": draw_pattern(jax.random.fold_in(splits[9], 71), 0),
        "time_qkv": draw_time_qkv(jax.random.fold_in(splits[9], 71), 0),
        "time_out": scatter_about(splits[6], (INNER, D), INNER ** -0.5, 0.25),
        "space_qkv": draw_space_qkv(jax.random.fold_in(splits[9], 71), 0),
        "space_out": scatter_about(splits[8], (INNER, D), INNER ** -0.5, 0.25),
    }


EPSILON = 1e-05
PRECISE = lax.Precision.HIGHEST

def normed(rows):
    values_f = rows.astype(jnp.float32)
    center = values_f - lax.optimization_barrier(jnp.mean(values_f, -1, keepdims=True))
    inv_std = lax.rsqrt(lax.optimization_barrier(jnp.mean(center * center, -1, keepdims=True)) + EPSILON)
    return (center * inv_std, inv_std)

def norm_back(rows, grad_in):
    normal_rows, inv_std = normed(rows)
    return inv_std * (grad_in - lax.optimization_barrier(jnp.mean(grad_in, -1, keepdims=True)) - normal_rows * lax.optimization_barrier(jnp.mean(grad_in * normal_rows, -1, keepdims=True)))

def matmul_f32(left, right):
    return jnp.dot(left, right, preferred_element_type=jnp.float32)

def matmul_tr(left, right):
    return lax.dot_general(left, right, (((left.ndim - 1,), (1,)), ((), ())), preferred_element_type=jnp.float32)

def contract(spec, left, right):
    return jnp.einsum(spec, left.astype(jnp.float32), right.astype(jnp.float32), precision=PRECISE)

def attend(queries, key_rows, value_rows, query_spec, key_spec, score_spec):
    factor = queries.shape[-1] ** (-0.5)
    scores = contract(query_spec + ',' + key_spec + '->' + score_spec, queries, key_rows) * factor
    weights = jax.nn.softmax(scores, axis=-1)
    mixed_rows = contract(score_spec + ',' + key_spec + '->' + query_spec, weights.astype(jnp.bfloat16), value_rows)
    return (mixed_rows.astype(jnp.bfloat16), weights)

def attend_back(queries, key_rows, value_rows, weights, out_grad, query_spec, key_spec, score_spec):
    factor = queries.shape[-1] ** (-0.5)
    value_grad = contract(score_spec + ',' + query_spec + '->' + key_spec, weights.astype(jnp.bfloat16), out_grad)
    weight_grad = contract(query_spec + ',' + key_spec + '->' + score_spec, out_grad, value_rows)
    row_delta = lax.optimization_barrier(jnp.sum(weights * weight_grad, -1, keepdims=True))
    score_grad = (weights * (weight_grad - row_delta)).astype(jnp.bfloat16)
    query_grad = contract(score_spec + ',' + key_spec + '->' + query_spec, score_grad, key_rows) * factor
    key_grad = contract(score_spec + ',' + query_spec + '->' + key_spec, score_grad, queries) * factor
    return (query_grad, key_grad, value_grad)

def reference(y_first, y_second, grad_first, grad_second, pattern, time_qkv, time_out, space_qkv, space_out):
    clips, frames, patches, unused_w = y_first.shape
    inner_w = time_out.shape[0]
    shard_count = patches // P_DEV

    def space_frame(inputs):
        rows, cotangent, beside = inputs
        normal_rows, unused = normed(rows)
        projected = matmul_f32(normal_rows.astype(jnp.bfloat16), space_qkv).astype(jnp.bfloat16)
        shards = projected.reshape(clips, shard_count, P_DEV, 3 * inner_w)
        own_ids = jnp.arange(shard_count, dtype=jnp.int32)
        block_ids = own_ids // 2
        neighbour = beside[block_ids].astype(jnp.int32)
        shard_ids = jnp.stack([2 * block_ids, 2 * block_ids + 1, 2 * neighbour, 2 * neighbour + 1], 1)
        window = shards[..., inner_w:][:, shard_ids]
        window = window.reshape(clips, shard_count, 4 * P_DEV, 2, HEADS, HEAD_DIM)
        queries = shards[..., :inner_w].reshape(clips, shard_count, P_DEV, HEADS, HEAD_DIM)
        key_rows = window[:, :, :, 0]
        value_rows = window[:, :, :, 1]
        mixed_rows, weights = attend(queries, key_rows, value_rows, 'cfqhe', 'cfkhe', 'cfhqk')
        value_out = matmul_f32(mixed_rows.reshape(clips, patches, inner_w), space_out)
        out_grad = matmul_tr(cotangent, space_out).astype(jnp.bfloat16)
        out_grad = out_grad.reshape(clips, shard_count, P_DEV, HEADS, HEAD_DIM)
        query_grad, key_grad, value_grad = attend_back(queries, key_rows, value_rows, weights, out_grad, 'cfqhe', 'cfkhe', 'cfhqk')
        slot_shape = (clips, shard_count, 4, P_DEV, inner_w)
        window_grad = jnp.concatenate([key_grad.astype(jnp.bfloat16).reshape(slot_shape), value_grad.astype(jnp.bfloat16).reshape(slot_shape)], -1)
        selector = (shard_ids[:, :, None] == own_ids[None, None, :]).astype(jnp.float32)
        summed = contract('qjs,cqjpx->cspx', selector, window_grad).astype(jnp.bfloat16)
        dqkv = jnp.concatenate([query_grad.astype(jnp.bfloat16).reshape(clips, shard_count, P_DEV, inner_w), summed], -1).reshape(clips, patches, 3 * inner_w)
        return (value_out, norm_back(rows, matmul_tr(dqkv, space_qkv)))
    space_value, space_norm = lax.map(space_frame, (jnp.moveaxis(y_first, 1, 0), jnp.moveaxis(grad_second, 1, 0), pattern))
    space_value = jnp.moveaxis(space_value, 0, 1)
    space_norm = jnp.moveaxis(space_norm, 0, 1)
    x_second = (y_second.astype(jnp.float32) - space_value).astype(jnp.bfloat16)
    normal_second, unused = normed(x_second)
    time_proj = matmul_f32(normal_second.astype(jnp.bfloat16), time_qkv).astype(jnp.bfloat16)
    split_rows = time_proj.reshape(clips, frames, patches, 3, HEADS, HEAD_DIM)
    time_mixed, time_weights = attend(split_rows[:, :, :, 0], split_rows[:, :, :, 1], split_rows[:, :, :, 2], 'cfphe', 'cgphe', 'cphfg')
    time_value = matmul_f32(time_mixed.reshape(clips, frames, patches, inner_w), time_out)
    x_first = (y_first.astype(jnp.float32) - time_value).astype(jnp.bfloat16)
    dx_first = (grad_first.astype(jnp.float32) + space_norm).astype(jnp.bfloat16)
    time_grad = matmul_tr(dx_first, time_out).astype(jnp.bfloat16)
    time_grad = time_grad.reshape(clips, frames, patches, HEADS, HEAD_DIM)
    time_grads = attend_back(split_rows[:, :, :, 0], split_rows[:, :, :, 1], split_rows[:, :, :, 2], time_weights, time_grad, 'cfphe', 'cgphe', 'cphfg')
    time_dqkv = jnp.stack(time_grads, 3).astype(jnp.bfloat16).reshape(clips, frames, patches, 3 * inner_w)
    dx_second = (grad_second.astype(jnp.float32) + norm_back(x_second, matmul_tr(time_dqkv, time_qkv))).astype(jnp.bfloat16)
    return (x_first, x_second, dx_first, dx_second)
```

```python
import functools

import jax
import jax.numpy as jnp
from jax import lax
from jax.experimental import pallas as pl
from jax.experimental.pallas import tpu as pltpu
from jax.sharding import PartitionSpec as P

HEADS = 8
HEAD_DIM = 64
INNER = HEADS * HEAD_DIM
EPSILON = 1e-05
FACTOR = HEAD_DIM ** (-0.5)
BF16 = jnp.bfloat16
F32 = jnp.float32


def normed(rows):
    values_f = rows.astype(F32)
    center = values_f - jnp.mean(values_f, -1, keepdims=True)
    inv_std = lax.rsqrt(jnp.mean(center * center, -1, keepdims=True) + EPSILON)
    return (center * inv_std, inv_std)


def norm_back(rows, grad_in):
    normal_rows, inv_std = normed(rows)
    return inv_std * (
        grad_in
        - jnp.mean(grad_in, -1, keepdims=True)
        - normal_rows * jnp.mean(grad_in * normal_rows, -1, keepdims=True)
    )


def mm(left, right):
    return jnp.dot(left, right, preferred_element_type=F32)


def mm_nt(left, right):
    return lax.dot_general(left, right, (((1,), (1,)), ((), ())), preferred_element_type=F32)


def mm_tn(left, right):
    return lax.dot_general(left, right, (((0,), (0,)), ((), ())), preferred_element_type=F32)


def low_lanes(shape):
    return lax.broadcasted_iota(jnp.int32, shape, len(shape) - 1) < HEAD_DIM


def split_halves(pair, low):
    zero = jnp.zeros_like(pair)
    return (jnp.where(low, pair, zero), jnp.where(low, zero, pair))


def softmax_grads(scores, weight_grad):
    top = jnp.max(scores, -1, keepdims=True)
    powers = jnp.exp(scores - top)
    weights = powers / jnp.sum(powers, -1, keepdims=True)
    row_delta = jnp.sum(weights * weight_grad, -1, keepdims=True)
    score_grad = (weights * (weight_grad - row_delta)).astype(BF16)
    return (weights.astype(BF16), score_grad)


def project_kernel(y_ref, grad_ref, qkv_ref, out_w_ref, send_ref):
    clips = send_ref.shape[0] // HEADS
    patches = send_ref.shape[1]
    normal, unused = normed(y_ref[...])
    proj = mm(normal.astype(BF16), qkv_ref[...])
    out_grad = mm_nt(grad_ref[...], out_w_ref[...])
    low = low_lanes((clips * patches, 2 * HEAD_DIM))
    for pair in range(HEADS // 2):
        cols = slice(2 * HEAD_DIM * pair, 2 * HEAD_DIM * (pair + 1))
        parts = [proj[:, INNER * i :][:, cols] for i in range(3)]
        queries, keys, values = parts
        grads = out_grad[:, cols]
        for half in range(2):
            tiles = []
            for left, right in ((queries, grads), (keys, values)):
                if half == 0:
                    tile = jnp.where(low, left, pltpu.roll(right, HEAD_DIM, 1))
                else:
                    tile = jnp.where(low, pltpu.roll(left, HEAD_DIM, 1), right)
                tiles.append(tile.astype(BF16))
            head = 2 * pair + half
            for clip in range(clips):
                rows = slice(patches * clip, patches * (clip + 1))
                for i in range(2):
                    send_ref[clip * HEADS + head, :, 128 * i : 128 * (i + 1)] = tiles[i][rows]


def space_kernel(pattern_ref, x_ref, out_ref, acc_ref):
    width = 2 * HEAD_DIM
    blocks = pattern_ref.shape[1]
    block = x_ref.shape[0] // blocks
    low_q = low_lanes((block, width))
    low_k = low_lanes((2 * block, width))
    scale = jnp.where(low_q, jnp.float32(FACTOR), jnp.float32(1.0))
    acc_ref[...] = jnp.zeros_like(acc_ref)
    for b in range(blocks):
        own = slice(block * b, block * (b + 1))
        beside = pl.ds(pl.multiple_of(pattern_ref[0, b] * block, block), block)
        query_rows = x_ref[own, :width]
        key_rows = jnp.concatenate([x_ref[own, width:], x_ref[beside, width:]], 0)
        q_low, g_high = split_halves(query_rows, low_q)
        k_low, v_high = split_halves(key_rows, low_k)
        stacked_q = jnp.concatenate([q_low, g_high], 0)
        both = mm_nt(stacked_q, key_rows)
        weights, score_grad = softmax_grads(both[:block] * FACTOR, both[block:])
        rows_out = mm(
            jnp.concatenate([score_grad, weights], 1), jnp.concatenate([k_low, v_high], 0)
        )
        out_ref[own, :width] = (rows_out * scale).astype(BF16)
        key_out = mm_tn(jnp.concatenate([score_grad, weights], 0), stacked_q)
        acc_ref[own, :] += key_out[:block]
        acc_ref[beside, :] += key_out[block:]
    for b in range(blocks):
        own = slice(block * b, block * (b + 1))
        out_ref[own, width:] = (acc_ref[own, :] * scale).astype(BF16)


def middle_kernel(
    recv_ref,
    y_first_ref,
    y_second_ref,
    grad_first_ref,
    space_qkv_ref,
    space_out_ref,
    time_out_ref,
    x_second_ref,
    dx_first_ref,
    send_ref,
):
    clips = recv_ref.shape[0] // HEADS
    patches = recv_ref.shape[1]
    low = low_lanes((patches, 2 * HEAD_DIM))
    sections = [[], [], [], []]
    for pair in range(HEADS // 2):
        made = [[], [], [], []]
        for clip in range(clips):
            at = clip * HEADS + 2 * pair
            for i in range(2):
                first = recv_ref[at, :, 128 * i : 128 * (i + 1)].astype(F32)
                second = recv_ref[at + 1, :, 128 * i : 128 * (i + 1)].astype(F32)
                made[2 * i].append(jnp.where(low, first, pltpu.roll(second, HEAD_DIM, 1)))
                made[2 * i + 1].append(jnp.where(low, pltpu.roll(first, HEAD_DIM, 1), second))
        for i in range(4):
            sections[i].append(jnp.concatenate(made[i], 0).astype(BF16))
    query_grad, mixed, key_grad, value_grad = [jnp.concatenate(s, 1) for s in sections]
    x_second = (y_second_ref[...].astype(F32) - mm(mixed, space_out_ref[...])).astype(BF16)
    x_second_ref[...] = x_second
    normal, unused = normed(x_second)
    send_ref[:, : x_second.shape[1]] = normal.astype(BF16)
    dqkv = jnp.concatenate([query_grad, key_grad, value_grad], 1)
    grad_in = mm_nt(dqkv, space_qkv_ref[...])
    dx_first = (
        grad_first_ref[...].astype(F32) + norm_back(y_first_ref[...], grad_in)
    ).astype(BF16)
    dx_first_ref[...] = dx_first
    send_ref[:, x_second.shape[1] :] = mm_nt(dx_first, time_out_ref[...]).astype(BF16)


def time_kernel(x_ref, qkv_ref, send_ref, *, sequences):
    rows = x_ref.shape[0]
    width = x_ref.shape[1] - INNER
    proj = mm(x_ref[:, :width], qkv_ref[...]).astype(BF16)
    lanes = 2 * HEAD_DIM
    low = low_lanes((rows, lanes))
    row_id = lax.broadcasted_iota(jnp.int32, (2 * rows, rows), 0)
    col_id = lax.broadcasted_iota(jnp.int32, (2 * rows, rows), 1)
    same = ((row_id ^ col_id) & (sequences - 1)) == 0
    lowest = jnp.finfo(jnp.float32).min
    sections = [[], [], []]
    for pair in range(HEADS // 2):
        at = lanes * pair
        queries = jnp.concatenate(split_halves(proj[:, at : at + lanes], low), 0)
        keys = proj[:, INNER + at : INNER + at + lanes]
        values = proj[:, 2 * INNER + at : 2 * INNER + at + lanes]
        grads = jnp.concatenate(
            split_halves(x_ref[:, width + at : width + at + lanes], low), 0
        )
        scores = jnp.where(same, mm_nt(queries, keys) * FACTOR, lowest)
        weights, score_grad = softmax_grads(scores, mm_nt(grads, values))
        keys_split = jnp.concatenate(split_halves(keys, low), 0)
        values_split = jnp.concatenate(split_halves(values, low), 0)
        mixed = mm(jnp.concatenate([weights[:rows], weights[rows:]], 1), values_split)
        send_ref[:, at : at + lanes] = mixed.astype(BF16)
        query_grad = mm(jnp.concatenate([score_grad[:rows], score_grad[rows:]], 1), keys_split)
        sections[0].append((query_grad * FACTOR).astype(BF16))
        sections[1].append((mm_tn(score_grad, queries) * FACTOR).astype(BF16))
        sections[2].append(mm_tn(weights, grads).astype(BF16))
    dqkv = jnp.concatenate(sections[0] + sections[1] + sections[2], 1)
    send_ref[:, INNER:] = mm_nt(dqkv, qkv_ref[...]).astype(BF16)


def last_kernel(recv_ref, y_first_ref, x_second_ref, grad_second_ref, out_w_ref, x_first_ref, dx_ref):
    value = mm(recv_ref[:, :INNER], out_w_ref[...])
    x_first_ref[...] = (y_first_ref[...].astype(F32) - value).astype(BF16)
    grad_in = recv_ref[:, INNER:].astype(F32)
    dx_ref[...] = (
        grad_second_ref[...].astype(F32) + norm_back(x_second_ref[...], grad_in)
    ).astype(BF16)


def shape_of(*sizes):
    return jax.ShapeDtypeStruct(sizes, BF16)


def exchange(rows, axis):
    return lax.all_to_all(rows, axis, split_axis=0, concat_axis=0, tiled=True)


def per_device(
    y_first, y_second, grad_first, grad_second, pattern, time_qkv, time_out, space_qkv, space_out
):
    shape = y_first.shape
    clips, unused, patches, width = shape
    rows = clips * patches
    flat = [a.reshape(rows, width) for a in (y_first, y_second, grad_first, grad_second)]
    y_first, y_second, grad_first, grad_second = flat
    groups = clips * HEADS
    head_cols = 4 * HEAD_DIM
    frames = lax.axis_size("tm")

    sent = pl.pallas_call(
        project_kernel, out_shape=shape_of(groups, patches, head_cols), name="project"
    )(y_first, grad_second, space_qkv, space_out)
    gathered = exchange(sent, "space").reshape(groups * patches, head_cols)
    space_rows = pl.pallas_call(
        space_kernel,
        out_shape=shape_of(groups * patches, head_cols),
        in_specs=[
            pl.BlockSpec(memory_space=pltpu.SMEM),
            pl.BlockSpec(memory_space=pltpu.VMEM),
        ],
        scratch_shapes=[pltpu.VMEM((groups * patches, 2 * HEAD_DIM), F32)],
        name="space_attention",
    )(pattern, gathered)
    returned = exchange(space_rows.reshape(groups, patches, head_cols), "space")
    x_second, dx_first, time_send = pl.pallas_call(
        middle_kernel,
        out_shape=(shape_of(rows, width), shape_of(rows, width), shape_of(rows, width + INNER)),
        name="middle",
    )(returned, y_first, y_second, grad_first, space_qkv, space_out, time_out)
    time_in = exchange(time_send.reshape(frames, rows // frames, width + INNER), "tm")
    time_rows = pl.pallas_call(
        functools.partial(time_kernel, sequences=rows // frames),
        out_shape=shape_of(rows, width + INNER),
        name="time_attention",
    )(time_in.reshape(rows, width + INNER), time_qkv)
    time_back = exchange(time_rows.reshape(frames, rows // frames, width + INNER), "tm")
    x_first, dx_second = pl.pallas_call(
        last_kernel, out_shape=(shape_of(rows, width), shape_of(rows, width)), name="last"
    )(time_back.reshape(rows, width + INNER), y_first, x_second, grad_second, time_out)
    return tuple(a.reshape(shape) for a in (x_first, x_second, dx_first, dx_second))


def solution(mesh):
    in_specs = (
        P(None, "tm", "space", None),
        P(None, "tm", "space", None),
        P(None, "tm", "space", None),
        P(None, "tm", "space", None),
        P("tm", None),
        P(),
        P(),
        P(),
        P(),
    )
    out_specs = (
        P(None, "tm", "space", None),
        P(None, "tm", "space", None),
        P(None, "tm", "space", None),
        P(None, "tm", "space", None),
    )
    return jax.shard_map(
        per_device, mesh=mesh, in_specs=in_specs, out_specs=out_specs, check_vma=False
    )
```

```python
import jax
import jax.numpy as jnp
from jax import lax
from jax.experimental import pallas as pl
from jax.experimental.pallas import tpu as pltpu
from jax.sharding import PartitionSpec as P

HEADS = 8
HEAD_DIM = 64
INNER = HEADS * HEAD_DIM
EPSILON = 1e-05
FACTOR = HEAD_DIM ** (-0.5)
BF16 = jnp.bfloat16
F32 = jnp.float32
PARAMS = pltpu.CompilerParams(vmem_limit_bytes=24 << 20)


def normed(rows):
    values_f = rows.astype(F32)
    center = values_f - jnp.mean(values_f, -1, keepdims=True)
    inv_std = lax.rsqrt(jnp.mean(center * center, -1, keepdims=True) + EPSILON)
    return (center * inv_std, inv_std)


def norm_back(rows, grad_in):
    normal_rows, inv_std = normed(rows)
    return inv_std * (
        grad_in
        - jnp.mean(grad_in, -1, keepdims=True)
        - normal_rows * jnp.mean(grad_in * normal_rows, -1, keepdims=True)
    )


def mm(left, right):
    return jnp.dot(left, right, preferred_element_type=F32)


def mm_nt(left, right):
    return lax.dot_general(left, right, (((1,), (1,)), ((), ())), preferred_element_type=F32)


def mm_tn(left, right):
    return lax.dot_general(left, right, (((0,), (0,)), ((), ())), preferred_element_type=F32)


def low_lanes(shape):
    return lax.broadcasted_iota(jnp.int32, shape, len(shape) - 1) < HEAD_DIM


def split_halves(pair, low):
    zero = jnp.zeros_like(pair)
    return (jnp.where(low, pair, zero), jnp.where(low, zero, pair))


def softmax_grads(scores, weight_grad):
    top = jnp.max(scores, -1, keepdims=True)
    powers = jnp.exp(scores - top)
    weights = powers / jnp.sum(powers, -1, keepdims=True)
    row_delta = jnp.sum(weights * weight_grad, -1, keepdims=True)
    score_grad = (weights * (weight_grad - row_delta)).astype(BF16)
    return (weights.astype(BF16), score_grad)


def project_kernel(y_ref, grad_ref, qkv_ref, out_w_ref, send_ref):
    clips = send_ref.shape[0] // HEADS
    patches = send_ref.shape[1]
    normal, unused = normed(y_ref[...])
    proj = mm(normal.astype(BF16), qkv_ref[...])
    out_grad = mm_nt(grad_ref[...], out_w_ref[...])
    low = low_lanes((clips * patches, 2 * HEAD_DIM))
    for pair in range(HEADS // 2):
        cols = slice(2 * HEAD_DIM * pair, 2 * HEAD_DIM * (pair + 1))
        parts = [proj[:, INNER * i :][:, cols] for i in range(3)]
        queries, keys, values = parts
        grads = out_grad[:, cols]
        for half in range(2):
            tiles = []
            for left, right in ((queries, grads), (keys, values)):
                if half == 0:
                    tile = jnp.where(low, left, pltpu.roll(right, HEAD_DIM, 1))
                else:
                    tile = jnp.where(low, pltpu.roll(left, HEAD_DIM, 1), right)
                tiles.append(tile.astype(BF16))
            head = 2 * pair + half
            for clip in range(clips):
                rows = slice(patches * clip, patches * (clip + 1))
                for i in range(2):
                    send_ref[clip * HEADS + head, :, 128 * i : 128 * (i + 1)] = tiles[i][rows]


def space_kernel(pattern_ref, x_ref, out_ref, acc_ref):
    width = 2 * HEAD_DIM
    blocks = pattern_ref.shape[1]
    block = x_ref.shape[0] // blocks
    low_q = low_lanes((block, width))
    low_k = low_lanes((2 * block, width))
    scale = jnp.where(low_q, jnp.float32(FACTOR), jnp.float32(1.0))
    acc_ref[...] = jnp.zeros_like(acc_ref)
    for b in range(blocks):
        own = slice(block * b, block * (b + 1))
        beside = pl.ds(pl.multiple_of(pattern_ref[0, b] * block, block), block)
        query_rows = x_ref[own, :width]
        key_rows = jnp.concatenate([x_ref[own, width:], x_ref[beside, width:]], 0)
        q_low, g_high = split_halves(query_rows, low_q)
        k_low, v_high = split_halves(key_rows, low_k)
        stacked_q = jnp.concatenate([q_low, g_high], 0)
        both = mm_nt(stacked_q, key_rows)
        weights, score_grad = softmax_grads(both[:block] * FACTOR, both[block:])
        rows_out = mm(
            jnp.concatenate([score_grad, weights], 1), jnp.concatenate([k_low, v_high], 0)
        )
        out_ref[own, :width] = (rows_out * scale).astype(BF16)
        key_out = mm_tn(jnp.concatenate([score_grad, weights], 0), stacked_q)
        acc_ref[own, :] += key_out[:block]
        acc_ref[beside, :] += key_out[block:]
    for b in range(blocks):
        own = slice(block * b, block * (b + 1))
        out_ref[own, width:] = (acc_ref[own, :] * scale).astype(BF16)


def middle_kernel(
    recv_ref,
    y_first_ref,
    y_second_ref,
    grad_first_ref,
    space_qkv_ref,
    space_out_ref,
    time_out_ref,
    x_second_ref,
    dx_first_ref,
    send_ref,
):
    clips = recv_ref.shape[0] // HEADS
    patches = recv_ref.shape[1]
    low = low_lanes((patches, 2 * HEAD_DIM))
    sections = [[], [], [], []]
    for pair in range(HEADS // 2):
        made = [[], [], [], []]
        for clip in range(clips):
            at = clip * HEADS + 2 * pair
            for i in range(2):
                first = recv_ref[at, :, 128 * i : 128 * (i + 1)].astype(F32)
                second = recv_ref[at + 1, :, 128 * i : 128 * (i + 1)].astype(F32)
                made[2 * i].append(jnp.where(low, first, pltpu.roll(second, HEAD_DIM, 1)))
                made[2 * i + 1].append(jnp.where(low, pltpu.roll(first, HEAD_DIM, 1), second))
        for i in range(4):
            sections[i].append(jnp.concatenate(made[i], 0).astype(BF16))
    query_grad, mixed, key_grad, value_grad = [jnp.concatenate(s, 1) for s in sections]
    x_second = (y_second_ref[...].astype(F32) - mm(mixed, space_out_ref[...])).astype(BF16)
    x_second_ref[...] = x_second
    normal, unused = normed(x_second)
    dqkv = jnp.concatenate([query_grad, key_grad, value_grad], 1)
    grad_in = mm_nt(dqkv, space_qkv_ref[...])
    dx_first = (
        grad_first_ref[...].astype(F32) + norm_back(y_first_ref[...], grad_in)
    ).astype(BF16)
    dx_first_ref[...] = dx_first
    time_grad = mm_nt(dx_first, time_out_ref[...]).astype(BF16)
    send_rows = jnp.concatenate([normal.astype(BF16), time_grad], 1)
    send_ref[...] = send_rows.reshape(send_ref.shape)


def time_kernel(x_ref, qkv_ref, send_ref, flat_ref):
    rows = x_ref.shape[0] * x_ref.shape[1]
    width = x_ref.shape[2] - INNER
    flat_ref[...] = x_ref[...].reshape(rows, width + INNER)
    proj = mm(flat_ref[:, :width], qkv_ref[...]).astype(BF16)
    lanes = 2 * HEAD_DIM
    low = low_lanes((rows, lanes))
    row_id = lax.broadcasted_iota(jnp.int32, (2 * rows, rows), 0)
    col_id = lax.broadcasted_iota(jnp.int32, (2 * rows, rows), 1)
    same = ((row_id ^ col_id) & (x_ref.shape[1] - 1)) == 0
    lowest = jnp.finfo(jnp.float32).min
    sections = [[], [], [], []]
    for pair in range(HEADS // 2):
        at = lanes * pair
        queries = jnp.concatenate(split_halves(proj[:, at : at + lanes], low), 0)
        keys = proj[:, INNER + at : INNER + at + lanes]
        values = proj[:, 2 * INNER + at : 2 * INNER + at + lanes]
        grads = jnp.concatenate(
            split_halves(flat_ref[:, width + at : width + at + lanes], low), 0
        )
        scores = jnp.where(same, mm_nt(queries, keys) * FACTOR, lowest)
        weights, score_grad = softmax_grads(scores, mm_nt(grads, values))
        keys_split = jnp.concatenate(split_halves(keys, low), 0)
        values_split = jnp.concatenate(split_halves(values, low), 0)
        mixed = mm(jnp.concatenate([weights[:rows], weights[rows:]], 1), values_split)
        sections[3].append(mixed.astype(BF16))
        query_grad = mm(jnp.concatenate([score_grad[:rows], score_grad[rows:]], 1), keys_split)
        sections[0].append((query_grad * FACTOR).astype(BF16))
        sections[1].append((mm_tn(score_grad, queries) * FACTOR).astype(BF16))
        sections[2].append(mm_tn(weights, grads).astype(BF16))
    dqkv = jnp.concatenate(sections[0] + sections[1] + sections[2], 1)
    grad_in = mm_nt(dqkv, qkv_ref[...]).astype(BF16)
    send_ref[...] = jnp.concatenate(sections[3] + [grad_in], 1).reshape(send_ref.shape)


def last_kernel(recv_ref, y_first_ref, x_second_ref, grad_second_ref, out_w_ref, x_first_ref, dx_ref):
    received = recv_ref[...].reshape(y_first_ref.shape[0], recv_ref.shape[2])
    value = mm(received[:, :INNER], out_w_ref[...])
    x_first_ref[...] = (y_first_ref[...].astype(F32) - value).astype(BF16)
    grad_in = received[:, INNER:].astype(F32)
    dx_ref[...] = (
        grad_second_ref[...].astype(F32) + norm_back(x_second_ref[...], grad_in)
    ).astype(BF16)


def shape_of(*sizes):
    return jax.ShapeDtypeStruct(sizes, BF16)


def exchange(rows, axis):
    return lax.all_to_all(rows, axis, split_axis=0, concat_axis=0, tiled=True)


def per_device(
    y_first, y_second, grad_first, grad_second, pattern, time_qkv, time_out, space_qkv, space_out
):
    shape = y_first.shape
    clips, unused, patches, width = shape
    rows = clips * patches
    flat = [a.reshape(rows, width) for a in (y_first, y_second, grad_first, grad_second)]
    y_first, y_second, grad_first, grad_second = flat
    groups = clips * HEADS
    head_cols = 4 * HEAD_DIM
    frames = lax.axis_size("tm")
    wire = (frames, rows // frames, width + INNER)

    sent = pl.pallas_call(
        project_kernel, out_shape=shape_of(groups, patches, head_cols), name="project", compiler_params=PARAMS
    )(y_first, grad_second, space_qkv, space_out)
    gathered = exchange(sent, "space").reshape(groups * patches, head_cols)
    space_rows = pl.pallas_call(
        space_kernel,
        out_shape=shape_of(groups * patches, head_cols),
        in_specs=[
            pl.BlockSpec(memory_space=pltpu.SMEM),
            pl.BlockSpec(memory_space=pltpu.VMEM),
        ],
        scratch_shapes=[pltpu.VMEM((groups * patches, 2 * HEAD_DIM), F32)],
        name="space_attention",
        compiler_params=PARAMS,
    )(pattern, gathered)
    returned = exchange(space_rows.reshape(groups, patches, head_cols), "space")
    x_second, dx_first, time_send = pl.pallas_call(
        middle_kernel,
        out_shape=(shape_of(rows, width), shape_of(rows, width), shape_of(*wire)),
        name="middle",
        compiler_params=PARAMS,
    )(returned, y_first, y_second, grad_first, space_qkv, space_out, time_out)
    time_rows = pl.pallas_call(
        time_kernel,
        out_shape=shape_of(*wire),
        scratch_shapes=[pltpu.VMEM((rows, width + INNER), BF16)],
        name="time_attention",
        compiler_params=PARAMS,
    )(exchange(time_send, "tm"), time_qkv)
    x_first, dx_second = pl.pallas_call(
        last_kernel,
        out_shape=(shape_of(rows, width), shape_of(rows, width)),
        name="last",
        compiler_params=PARAMS,
    )(exchange(time_rows, "tm"), y_first, x_second, grad_second, time_out)
    return tuple(a.reshape(shape) for a in (x_first, x_second, dx_first, dx_second))


def solution(mesh):
    in_specs = (
        P(None, "tm", "space", None),
        P(None, "tm", "space", None),
        P(None, "tm", "space", None),
        P(None, "tm", "space", None),
        P("tm", None),
        P(),
        P(),
        P(),
        P(),
    )
    out_specs = (
        P(None, "tm", "space", None),
        P(None, "tm", "space", None),
        P(None, "tm", "space", None),
        P(None, "tm", "space", None),
    )
    return jax.shard_map(
        per_device, mesh=mesh, in_specs=in_specs, out_specs=out_specs, check_vma=False
    )
```

```python
import jax
import jax.numpy as jnp
from jax import lax
from jax.experimental import pallas as pl
from jax.experimental.pallas import tpu as pltpu
from jax.sharding import PartitionSpec as P

HEADS = 8
HEAD_DIM = 64
INNER = HEADS * HEAD_DIM
EPSILON = 1e-05
FACTOR = HEAD_DIM ** (-0.5)
BF16 = jnp.bfloat16
F32 = jnp.float32
PARAMS = pltpu.CompilerParams(vmem_limit_bytes=24 << 20)


def normed(rows):
    values_f = rows.astype(F32)
    center = values_f - jnp.mean(values_f, -1, keepdims=True)
    inv_std = lax.rsqrt(jnp.mean(center * center, -1, keepdims=True) + EPSILON)
    return (center * inv_std, inv_std)


def norm_back(rows, grad_in):
    normal_rows, inv_std = normed(rows)
    return inv_std * (
        grad_in
        - jnp.mean(grad_in, -1, keepdims=True)
        - normal_rows * jnp.mean(grad_in * normal_rows, -1, keepdims=True)
    )


def mm(left, right):
    return jnp.dot(left, right, preferred_element_type=F32)


def mm_nt(left, right):
    return lax.dot_general(left, right, (((1,), (1,)), ((), ())), preferred_element_type=F32)


def mm_tn(left, right):
    return lax.dot_general(left, right, (((0,), (0,)), ((), ())), preferred_element_type=F32)


def low_lanes(shape):
    return lax.broadcasted_iota(jnp.int32, shape, len(shape) - 1) < HEAD_DIM


def split_halves(pair, low):
    zero = jnp.zeros_like(pair)
    return (jnp.where(low, pair, zero), jnp.where(low, zero, pair))


def softmax_grads(scores, weight_grad):
    top = jnp.max(scores, 0, keepdims=True)
    powers = jnp.exp(scores - top)
    weights = powers * (1.0 / jnp.sum(powers, 0, keepdims=True))
    row_delta = jnp.sum(weights * weight_grad, 0, keepdims=True)
    score_grad = (weights * (weight_grad - row_delta)).astype(BF16)
    return (weights.astype(BF16), score_grad)


def project_kernel(
    y_hbm, grad_hbm, qkv_hbm, out_w_hbm, send_ref, qkv_ref, out_w_ref, y_ref, grad_ref, sems
):
    clips = send_ref.shape[0] // HEADS
    patches = send_ref.shape[1]
    pairs = [(y_hbm, y_ref), (grad_hbm, grad_ref), (out_w_hbm, out_w_ref)]
    for i in range(3):
        cols = pl.ds(INNER * i, INNER)
        pairs.append((qkv_hbm.at[:, cols], qkv_ref.at[:, cols]))
    copies = [
        pltpu.make_async_copy(source, target, sems.at[i])
        for i, (source, target) in enumerate(pairs)
    ]
    for copy in copies:
        copy.start()
    copies[0].wait()
    normal = normed(y_ref[...])[0].astype(BF16)
    copies[1].wait()
    copies[2].wait()
    out_grad = mm_nt(grad_ref[...], out_w_ref[...])
    proj = []
    for i in range(3):
        copies[3 + i].wait()
        proj.append(mm(normal, qkv_ref[:, INNER * i : INNER * (i + 1)]))
    low = low_lanes((clips * patches, 2 * HEAD_DIM))
    for pair in range(HEADS // 2):
        cols = slice(2 * HEAD_DIM * pair, 2 * HEAD_DIM * (pair + 1))
        queries, keys, values = [part[:, cols] for part in proj]
        grads = out_grad[:, cols]
        for half in range(2):
            tiles = []
            for left, right in ((queries, grads), (keys, values)):
                if half == 0:
                    tile = jnp.where(low, left, pltpu.roll(right, HEAD_DIM, 1))
                else:
                    tile = jnp.where(low, pltpu.roll(left, HEAD_DIM, 1), right)
                tiles.append(tile.astype(BF16))
            head = 2 * pair + half
            for clip in range(clips):
                rows = slice(patches * clip, patches * (clip + 1))
                for i in range(2):
                    send_ref[clip * HEADS + head, :, 128 * i : 128 * (i + 1)] = tiles[i][rows]


def space_kernel(pattern_ref, x_ref, out_ref, both_ref, grads_ref, own_ref, beside_ref):
    width = 2 * HEAD_DIM
    blocks = pattern_ref.shape[1]
    block = x_ref.shape[0] // blocks
    low_q = low_lanes((block, width))
    low_k = low_lanes((2 * block, width))
    scale = jnp.where(low_q, jnp.float32(FACTOR), jnp.float32(1.0))

    def rows_of(b):
        return slice(block * b, block * (b + 1))

    def stacked_queries(b):
        return jnp.concatenate(split_halves(x_ref[rows_of(b), :width], low_q), 0)

    def key_rows(b):
        beside = pl.ds(pl.multiple_of(pattern_ref[0, b] * block, block), block)
        return jnp.concatenate([x_ref[rows_of(b), width:], x_ref[beside, width:]], 0)

    def score(b):
        both_ref[b] = mm_nt(key_rows(b), stacked_queries(b))

    def weigh(b):
        weights, score_grad = softmax_grads(both_ref[b, :, :block] * FACTOR, both_ref[b, :, block:])
        grads_ref[b, :, :block] = score_grad
        grads_ref[b, :, block:] = weights

    def spread(b):
        k_low, v_high = split_halves(key_rows(b), low_k)
        rows_out = mm_tn(grads_ref[b, :, :block], k_low) + mm_tn(grads_ref[b, :, block:], v_high)
        out_ref[rows_of(b), :width] = (rows_out * scale).astype(BF16)
        key_out = mm(grads_ref[b], stacked_queries(b))
        own_ref[rows_of(b), :] = key_out[:block]
        beside_ref[rows_of(b), :] = key_out[block:]

    for step in range(blocks + 2):
        for stage, lag in ((score, 0), (weigh, 1), (spread, 2)):
            if 0 <= step - lag < blocks:
                stage(step - lag)
    for b in range(blocks):
        total = own_ref[rows_of(b), :]
        for other in range(max(b - 1, 0), min(b + 2, blocks)):
            part = beside_ref[rows_of(other), :]
            total = total + jnp.where(pattern_ref[0, other] == b, part, 0.0)
        out_ref[rows_of(b), width:] = (total * scale).astype(BF16)


def middle_kernel(
    recv_ref,
    y_first_ref,
    y_second_ref,
    grad_first_ref,
    space_qkv_ref,
    space_out_ref,
    time_out_ref,
    x_second_ref,
    dx_first_ref,
    send_ref,
):
    clips = recv_ref.shape[0] // HEADS
    patches = recv_ref.shape[1]
    low = low_lanes((patches, 2 * HEAD_DIM))
    sections = [[], [], [], []]
    for pair in range(HEADS // 2):
        made = [[], [], [], []]
        for clip in range(clips):
            at = clip * HEADS + 2 * pair
            for i in range(2):
                first = recv_ref[at, :, 128 * i : 128 * (i + 1)].astype(F32)
                second = recv_ref[at + 1, :, 128 * i : 128 * (i + 1)].astype(F32)
                made[2 * i].append(jnp.where(low, first, pltpu.roll(second, HEAD_DIM, 1)))
                made[2 * i + 1].append(jnp.where(low, pltpu.roll(first, HEAD_DIM, 1), second))
        for i in range(4):
            sections[i].append(jnp.concatenate(made[i], 0).astype(BF16))
    query_grad, mixed, key_grad, value_grad = [jnp.concatenate(s, 1) for s in sections]
    x_second = (y_second_ref[...].astype(F32) - mm(mixed, space_out_ref[...])).astype(BF16)
    x_second_ref[...] = x_second
    normal, unused = normed(x_second)
    dqkv = jnp.concatenate([query_grad, key_grad, value_grad], 1)
    grad_in = mm_nt(dqkv, space_qkv_ref[...])
    dx_first = (
        grad_first_ref[...].astype(F32) + norm_back(y_first_ref[...], grad_in)
    ).astype(BF16)
    dx_first_ref[...] = dx_first
    time_grad = mm_nt(dx_first, time_out_ref[...]).astype(BF16)
    send_rows = jnp.concatenate([normal.astype(BF16), time_grad], 1)
    send_ref[...] = send_rows.reshape(send_ref.shape)


def time_kernel(x_ref, qkv_ref, send_ref, flat_ref):
    rows = x_ref.shape[0] * x_ref.shape[1]
    width = x_ref.shape[2] - INNER
    flat_ref[...] = x_ref[...].reshape(rows, width + INNER)
    proj = mm(flat_ref[:, :width], qkv_ref[...]).astype(BF16)
    lanes = 2 * HEAD_DIM
    low = low_lanes((rows, lanes))
    row_id = lax.broadcasted_iota(jnp.int32, (rows, 2 * rows), 0)
    col_id = lax.broadcasted_iota(jnp.int32, (rows, 2 * rows), 1)
    same = ((row_id ^ col_id) & (x_ref.shape[1] - 1)) == 0
    lowest = jnp.finfo(jnp.float32).min
    sections = [[], [], [], []]
    for pair in range(HEADS // 2):
        at = lanes * pair
        queries = jnp.concatenate(split_halves(proj[:, at : at + lanes], low), 0)
        keys = proj[:, INNER + at : INNER + at + lanes]
        values = proj[:, 2 * INNER + at : 2 * INNER + at + lanes]
        grads = jnp.concatenate(
            split_halves(flat_ref[:, width + at : width + at + lanes], low), 0
        )
        scores = jnp.where(same, mm_nt(keys, queries) * FACTOR, lowest)
        weights, score_grad = softmax_grads(scores, mm_nt(values, grads))
        keys_split = jnp.concatenate(split_halves(keys, low), 0)
        values_split = jnp.concatenate(split_halves(values, low), 0)
        mixed = mm_tn(jnp.concatenate([weights[:, :rows], weights[:, rows:]], 0), values_split)
        sections[3].append(mixed.astype(BF16))
        query_grad = mm_tn(
            jnp.concatenate([score_grad[:, :rows], score_grad[:, rows:]], 0), keys_split
        )
        sections[0].append((query_grad * FACTOR).astype(BF16))
        sections[1].append((mm(score_grad, queries) * FACTOR).astype(BF16))
        sections[2].append(mm(weights, grads).astype(BF16))
    dqkv = jnp.concatenate(sections[0] + sections[1] + sections[2], 1)
    grad_in = mm_nt(dqkv, qkv_ref[...]).astype(BF16)
    send_ref[...] = jnp.concatenate(sections[3] + [grad_in], 1).reshape(send_ref.shape)


def last_kernel(recv_ref, y_first_ref, x_second_ref, grad_second_ref, out_w_ref, x_first_ref, dx_ref):
    received = recv_ref[...].reshape(y_first_ref.shape[0], recv_ref.shape[2])
    value = mm(received[:, :INNER], out_w_ref[...])
    x_first_ref[...] = (y_first_ref[...].astype(F32) - value).astype(BF16)
    grad_in = received[:, INNER:].astype(F32)
    dx_ref[...] = (
        grad_second_ref[...].astype(F32) + norm_back(x_second_ref[...], grad_in)
    ).astype(BF16)


def shape_of(*sizes):
    return jax.ShapeDtypeStruct(sizes, BF16)


def exchange(rows, axis):
    return lax.all_to_all(rows, axis, split_axis=0, concat_axis=0, tiled=True)


def per_device(
    y_first, y_second, grad_first, grad_second, pattern, time_qkv, time_out, space_qkv, space_out
):
    shape = y_first.shape
    clips, unused, patches, width = shape
    rows = clips * patches
    flat = [a.reshape(rows, width) for a in (y_first, y_second, grad_first, grad_second)]
    y_first, y_second, grad_first, grad_second = flat
    groups = clips * HEADS
    head_cols = 4 * HEAD_DIM
    blocks = pattern.shape[1]
    block = groups * patches // blocks
    frames = lax.axis_size("tm")
    wire = (frames, rows // frames, width + INNER)

    hbm = pl.BlockSpec(memory_space=pltpu.HBM)
    sent, space_qkv, space_out = pl.pallas_call(
        project_kernel,
        out_shape=(
            shape_of(groups, patches, head_cols),
            shape_of(*space_qkv.shape),
            shape_of(*space_out.shape),
        ),
        in_specs=[hbm] * 4,
        scratch_shapes=[
            pltpu.VMEM((rows, width), BF16),
            pltpu.VMEM((rows, width), BF16),
            pltpu.SemaphoreType.DMA((6,)),
        ],
        name="project",
        compiler_params=PARAMS,
    )(
        *[
            pltpu.with_memory_space_constraint(a, pltpu.HBM)
            for a in (y_first, grad_second, space_qkv, space_out)
        ]
    )
    gathered = exchange(sent, "space").reshape(groups * patches, head_cols)
    space_rows = pl.pallas_call(
        space_kernel,
        out_shape=shape_of(groups * patches, head_cols),
        in_specs=[
            pl.BlockSpec(memory_space=pltpu.SMEM),
            pl.BlockSpec(memory_space=pltpu.VMEM),
        ],
        scratch_shapes=[
            pltpu.VMEM((blocks, 2 * block, 2 * block), F32),
            pltpu.VMEM((blocks, 2 * block, 2 * block), BF16),
            pltpu.VMEM((groups * patches, 2 * HEAD_DIM), F32),
            pltpu.VMEM((groups * patches, 2 * HEAD_DIM), F32),
        ],
        name="space_attention",
        compiler_params=PARAMS,
    )(pattern, gathered)
    returned = exchange(space_rows.reshape(groups, patches, head_cols), "space")
    x_second, dx_first, time_send = pl.pallas_call(
        middle_kernel,
        out_shape=(shape_of(rows, width), shape_of(rows, width), shape_of(*wire)),
        name="middle",
        compiler_params=PARAMS,
    )(returned, y_first, y_second, grad_first, space_qkv, space_out, time_out)
    time_rows = pl.pallas_call(
        time_kernel,
        out_shape=shape_of(*wire),
        scratch_shapes=[pltpu.VMEM((rows, width + INNER), BF16)],
        name="time_attention",
        compiler_params=PARAMS,
    )(exchange(time_send, "tm"), time_qkv)
    x_first, dx_second = pl.pallas_call(
        last_kernel,
        out_shape=(shape_of(rows, width), shape_of(rows, width)),
        name="last",
        compiler_params=PARAMS,
    )(exchange(time_rows, "tm"), y_first, x_second, grad_second, time_out)
    return tuple(a.reshape(shape) for a in (x_first, x_second, dx_first, dx_second))


def solution(mesh):
    in_specs = (
        P(None, "tm", "space", None),
        P(None, "tm", "space", None),
        P(None, "tm", "space", None),
        P(None, "tm", "space", None),
        P("tm", None),
        P(),
        P(),
        P(),
        P(),
    )
    out_specs = (
        P(None, "tm", "space", None),
        P(None, "tm", "space", None),
        P(None, "tm", "space", None),
        P(None, "tm", "space", None),
    )
    return jax.shard_map(
        per_device, mesh=mesh, in_specs=in_specs, out_specs=out_specs, check_vma=False
    )
```

```python
import jax
import jax.numpy as jnp
from jax import lax
from jax.experimental import pallas as pl
from jax.experimental.pallas import tpu as pltpu
from jax.sharding import PartitionSpec as P

HEADS = 8
HEAD_DIM = 64
INNER = HEADS * HEAD_DIM
EPSILON = 1e-05
FACTOR = HEAD_DIM ** (-0.5)
BF16 = jnp.bfloat16
F32 = jnp.float32
PARAMS = pltpu.CompilerParams(vmem_limit_bytes=24 << 20)


def normed(rows):
    values_f = rows.astype(F32)
    center = values_f - jnp.mean(values_f, -1, keepdims=True)
    inv_std = lax.rsqrt(jnp.mean(center * center, -1, keepdims=True) + EPSILON)
    return (center * inv_std, inv_std)


def norm_back(normal_rows, inv_std, grad_in):
    return inv_std * (
        grad_in
        - jnp.mean(grad_in, -1, keepdims=True)
        - normal_rows * jnp.mean(grad_in * normal_rows, -1, keepdims=True)
    )


def mm(left, right):
    return jnp.dot(left, right, preferred_element_type=F32)


def mm_nt(left, right):
    return lax.dot_general(left, right, (((1,), (1,)), ((), ())), preferred_element_type=F32)


def mm_tn(left, right):
    return lax.dot_general(left, right, (((0,), (0,)), ((), ())), preferred_element_type=F32)


def low_lanes(shape):
    return lax.broadcasted_iota(jnp.int32, shape, len(shape) - 1) < HEAD_DIM


def split_halves(pair, low):
    zero = jnp.zeros_like(pair)
    return (jnp.where(low, pair, zero), jnp.where(low, zero, pair))


def softmax_grads(scores, weight_grad):
    top = jnp.max(scores, 0, keepdims=True)
    powers = jnp.exp(scores - top)
    weights = powers * (1.0 / jnp.sum(powers, 0, keepdims=True))
    row_delta = jnp.sum(weights * weight_grad, 0, keepdims=True)
    score_grad = (weights * (weight_grad - row_delta)).astype(BF16)
    return (weights.astype(BF16), score_grad)


def project_kernel(
    y_hbm,
    grad_hbm,
    qkv_hbm,
    out_w_hbm,
    send_ref,
    qkv_ref,
    out_w_ref,
    normal_ref,
    std_ref,
    y_ref,
    grad_ref,
    sems,
):
    clips = send_ref.shape[0] // HEADS
    patches = send_ref.shape[1]
    pairs = [(y_hbm, y_ref), (grad_hbm, grad_ref), (out_w_hbm, out_w_ref)]
    for i in range(3):
        cols = pl.ds(INNER * i, INNER)
        pairs.append((qkv_hbm.at[:, cols], qkv_ref.at[:, cols]))
    copies = [
        pltpu.make_async_copy(source, target, sems.at[i])
        for i, (source, target) in enumerate(pairs)
    ]
    for copy in copies:
        copy.start()
    copies[0].wait()
    normal, inv_std = normed(y_ref[...])
    normal_ref[...] = normal
    std_ref[...] = jnp.broadcast_to(inv_std, std_ref.shape)
    normal = normal.astype(BF16)
    copies[1].wait()
    copies[2].wait()
    out_grad = mm_nt(grad_ref[...], out_w_ref[...])
    low = low_lanes((clips * patches, 2 * HEAD_DIM))

    def assemble(lefts, rights, part):
        for pair in range(HEADS // 2):
            cols = slice(2 * HEAD_DIM * pair, 2 * HEAD_DIM * (pair + 1))
            left, right = lefts[:, cols], rights[:, cols]
            tiles = (
                jnp.where(low, left, pltpu.roll(right, HEAD_DIM, 1)),
                jnp.where(low, pltpu.roll(left, HEAD_DIM, 1), right),
            )
            for half in range(2):
                tile = tiles[half].astype(BF16)
                for clip in range(clips):
                    send_ref[clip * HEADS + 2 * pair + half, :, 128 * part : 128 * (part + 1)] = (
                        tile[patches * clip : patches * (clip + 1)]
                    )

    def projected(i):
        copies[3 + i].wait()
        return mm(normal, qkv_ref[:, INNER * i : INNER * (i + 1)])

    assemble(projected(0), out_grad, 0)
    keys = projected(1)
    assemble(keys, projected(2), 1)


def space_kernel(pattern_ref, x_ref, out_ref, both_ref, grads_ref, own_ref, beside_ref):
    width = 2 * HEAD_DIM
    blocks = pattern_ref.shape[1]
    block = x_ref.shape[0] // blocks
    low_q = low_lanes((block, width))
    low_k = low_lanes((2 * block, width))
    scale = jnp.where(low_q, jnp.float32(FACTOR), jnp.float32(1.0))

    def rows_of(b):
        return slice(block * b, block * (b + 1))

    def stacked_queries(b):
        return jnp.concatenate(split_halves(x_ref[rows_of(b), :width], low_q), 0)

    def key_rows(b):
        beside = pl.ds(pl.multiple_of(pattern_ref[0, b] * block, block), block)
        return jnp.concatenate([x_ref[rows_of(b), width:], x_ref[beside, width:]], 0)

    def score(b):
        both_ref[b] = mm_nt(key_rows(b), stacked_queries(b))

    def weigh(b):
        weights, score_grad = softmax_grads(both_ref[b, :, :block] * FACTOR, both_ref[b, :, block:])
        grads_ref[b, :, :block] = score_grad
        grads_ref[b, :, block:] = weights

    def spread(b):
        k_low, v_high = split_halves(key_rows(b), low_k)
        rows_out = mm_tn(grads_ref[b, :, :block], k_low) + mm_tn(grads_ref[b, :, block:], v_high)
        out_ref[rows_of(b), :width] = (rows_out * scale).astype(BF16)
        key_out = mm(grads_ref[b], stacked_queries(b))
        own_ref[rows_of(b), :] = key_out[:block]
        beside_ref[rows_of(b), :] = key_out[block:]

    for step in range(blocks + 2):
        for stage, lag in ((score, 0), (weigh, 1), (spread, 2)):
            if 0 <= step - lag < blocks:
                stage(step - lag)
    for b in range(blocks):
        total = own_ref[rows_of(b), :]
        for other in range(max(b - 1, 0), min(b + 2, blocks)):
            part = beside_ref[rows_of(other), :]
            total = total + jnp.where(pattern_ref[0, other] == b, part, 0.0)
        out_ref[rows_of(b), width:] = (total * scale).astype(BF16)


def middle_kernel(
    recv_ref,
    normal_first_ref,
    std_first_ref,
    y_second_ref,
    grad_first_ref,
    space_qkv_ref,
    space_out_ref,
    time_out_ref,
    x_second_ref,
    dx_first_ref,
    send_ref,
    normal_ref,
    std_ref,
):
    clips = recv_ref.shape[0] // HEADS
    patches = recv_ref.shape[1]
    low = low_lanes((patches, 2 * HEAD_DIM))
    sections = [[], [], [], []]
    for pair in range(HEADS // 2):
        made = [[], [], [], []]
        for clip in range(clips):
            at = clip * HEADS + 2 * pair
            for i in range(2):
                first = recv_ref[at, :, 128 * i : 128 * (i + 1)].astype(F32)
                second = recv_ref[at + 1, :, 128 * i : 128 * (i + 1)].astype(F32)
                made[2 * i].append(jnp.where(low, first, pltpu.roll(second, HEAD_DIM, 1)))
                made[2 * i + 1].append(jnp.where(low, pltpu.roll(first, HEAD_DIM, 1), second))
        for i in range(4):
            sections[i].append(jnp.concatenate(made[i], 0).astype(BF16))
    query_grad, mixed, key_grad, value_grad = [jnp.concatenate(s, 1) for s in sections]
    x_second = (y_second_ref[...].astype(F32) - mm(mixed, space_out_ref[...])).astype(BF16)
    x_second_ref[...] = x_second
    normal, inv_std = normed(x_second)
    normal_ref[...] = normal
    std_ref[...] = jnp.broadcast_to(inv_std, std_ref.shape)
    dqkv = jnp.concatenate([query_grad, key_grad, value_grad], 1)
    grad_in = mm_nt(dqkv, space_qkv_ref[...])
    grad_in = norm_back(normal_first_ref[...], std_first_ref[:, :1], grad_in)
    dx_first = (grad_first_ref[...].astype(F32) + grad_in).astype(BF16)
    dx_first_ref[...] = dx_first
    time_grad = mm_nt(dx_first, time_out_ref[...]).astype(BF16)
    send_rows = jnp.concatenate([normal.astype(BF16), time_grad], 1)
    send_ref[...] = send_rows.reshape(send_ref.shape)


def time_kernel(x_ref, qkv_ref, send_ref, flat_ref, proj_ref, both_ref, grads_ref, dqkv_ref):
    rows = x_ref.shape[0] * x_ref.shape[1]
    width = x_ref.shape[2] - INNER
    flat_ref[...] = x_ref[...].reshape(rows, width + INNER)
    for i in range(3):
        cols = slice(INNER * i, INNER * (i + 1))
        proj_ref[:, cols] = mm(flat_ref[:, :width], qkv_ref[:, cols]).astype(BF16)
    lanes = 2 * HEAD_DIM
    low = low_lanes((rows, lanes))
    row_id = lax.broadcasted_iota(jnp.int32, (rows, 2 * rows), 0)
    col_id = lax.broadcasted_iota(jnp.int32, (rows, 2 * rows), 1)
    same = ((row_id ^ col_id) & (x_ref.shape[1] - 1)) == 0
    lowest = jnp.finfo(jnp.float32).min
    pairs = HEADS // 2
    mixed_parts = []

    def split_rows(ref, start, pair):
        at = start + lanes * pair
        return jnp.concatenate(split_halves(ref[:, at : at + lanes], low), 0)

    def score(pair):
        at = lanes * pair
        keys = proj_ref[:, INNER + at : INNER + at + lanes]
        values = proj_ref[:, 2 * INNER + at : 2 * INNER + at + lanes]
        both_ref[pair, :, : 2 * rows] = mm_nt(keys, split_rows(proj_ref, 0, pair))
        both_ref[pair, :, 2 * rows :] = mm_nt(values, split_rows(flat_ref, width, pair))

    def weigh(pair):
        scores = jnp.where(same, both_ref[pair, :, : 2 * rows] * FACTOR, lowest)
        weights, score_grad = softmax_grads(scores, both_ref[pair, :, 2 * rows :])
        grads_ref[pair, :, : 2 * rows] = score_grad
        grads_ref[pair, :, 2 * rows :] = weights

    def spread(pair):
        at = lanes * pair
        score_grad = grads_ref[pair, :, : 2 * rows]
        weights = grads_ref[pair, :, 2 * rows :]
        mixed = mm_tn(
            jnp.concatenate([weights[:, :rows], weights[:, rows:]], 0),
            split_rows(proj_ref, 2 * INNER, pair),
        )
        mixed_parts.append(mixed.astype(BF16))
        query_grad = mm_tn(
            jnp.concatenate([score_grad[:, :rows], score_grad[:, rows:]], 0),
            split_rows(proj_ref, INNER, pair),
        )
        key_grad = mm(score_grad, split_rows(proj_ref, 0, pair))
        value_grad = mm(weights, split_rows(flat_ref, width, pair))
        dqkv_ref[:, at : at + lanes] = (query_grad * FACTOR).astype(BF16)
        dqkv_ref[:, INNER + at : INNER + at + lanes] = (key_grad * FACTOR).astype(BF16)
        dqkv_ref[:, 2 * INNER + at : 2 * INNER + at + lanes] = value_grad.astype(BF16)

    for step in range(pairs + 2):
        for stage, lag in ((score, 0), (weigh, 1), (spread, 2)):
            if 0 <= step - lag < pairs:
                stage(step - lag)
    grad_in = mm_nt(dqkv_ref[...], qkv_ref[...]).astype(BF16)
    send_ref[...] = jnp.concatenate(mixed_parts + [grad_in], 1).reshape(send_ref.shape)


def last_kernel(
    recv_ref, y_first_ref, normal_ref, std_ref, grad_second_ref, out_w_ref, x_first_ref, dx_ref
):
    received = recv_ref[...].reshape(y_first_ref.shape[0], recv_ref.shape[2])
    value = mm(received[:, :INNER], out_w_ref[...])
    x_first_ref[...] = (y_first_ref[...].astype(F32) - value).astype(BF16)
    grad_in = received[:, INNER:].astype(F32)
    grad_in = norm_back(normal_ref[...], std_ref[:, :1], grad_in)
    dx_ref[...] = (grad_second_ref[...].astype(F32) + grad_in).astype(BF16)


def shape_of(*sizes):
    return jax.ShapeDtypeStruct(sizes, BF16)


def exchange(rows, axis):
    return lax.all_to_all(rows, axis, split_axis=0, concat_axis=0, tiled=True)


def per_device(
    y_first, y_second, grad_first, grad_second, pattern, time_qkv, time_out, space_qkv, space_out
):
    shape = y_first.shape
    clips, unused, patches, width = shape
    rows = clips * patches
    flat = [a.reshape(rows, width) for a in (y_first, y_second, grad_first, grad_second)]
    y_first, y_second, grad_first, grad_second = flat
    groups = clips * HEADS
    head_cols = 4 * HEAD_DIM
    blocks = pattern.shape[1]
    block = groups * patches // blocks
    frames = lax.axis_size("tm")
    wire = (frames, rows // frames, width + INNER)

    hbm = pl.BlockSpec(memory_space=pltpu.HBM)
    norm_shapes = (
        jax.ShapeDtypeStruct((rows, width), F32),
        jax.ShapeDtypeStruct((rows, 128), F32),
    )
    sent, space_qkv, space_out, normal_first, std_first = pl.pallas_call(
        project_kernel,
        out_shape=(
            shape_of(groups, patches, head_cols),
            shape_of(*space_qkv.shape),
            shape_of(*space_out.shape),
            *norm_shapes,
        ),
        in_specs=[hbm] * 4,
        scratch_shapes=[
            pltpu.VMEM((rows, width), BF16),
            pltpu.VMEM((rows, width), BF16),
            pltpu.SemaphoreType.DMA((6,)),
        ],
        name="project",
        compiler_params=PARAMS,
    )(
        *[
            pltpu.with_memory_space_constraint(a, pltpu.HBM)
            for a in (y_first, grad_second, space_qkv, space_out)
        ]
    )
    gathered = exchange(sent, "space").reshape(groups * patches, head_cols)
    space_rows = pl.pallas_call(
        space_kernel,
        out_shape=shape_of(groups * patches, head_cols),
        in_specs=[
            pl.BlockSpec(memory_space=pltpu.SMEM),
            pl.BlockSpec(memory_space=pltpu.VMEM),
        ],
        scratch_shapes=[
            pltpu.VMEM((blocks, 2 * block, 2 * block), F32),
            pltpu.VMEM((blocks, 2 * block, 2 * block), BF16),
            pltpu.VMEM((groups * patches, 2 * HEAD_DIM), F32),
            pltpu.VMEM((groups * patches, 2 * HEAD_DIM), F32),
        ],
        name="space_attention",
        compiler_params=PARAMS,
    )(pattern, gathered)
    returned = exchange(space_rows.reshape(groups, patches, head_cols), "space")
    x_second, dx_first, time_send, normal_second, std_second = pl.pallas_call(
        middle_kernel,
        out_shape=(shape_of(rows, width), shape_of(rows, width), shape_of(*wire), *norm_shapes),
        name="middle",
        compiler_params=PARAMS,
    )(returned, normal_first, std_first, y_second, grad_first, space_qkv, space_out, time_out)
    time_rows = pl.pallas_call(
        time_kernel,
        out_shape=shape_of(*wire),
        scratch_shapes=[
            pltpu.VMEM((rows, width + INNER), BF16),
            pltpu.VMEM((rows, 3 * INNER), BF16),
            pltpu.VMEM((HEADS // 2, rows, 4 * rows), F32),
            pltpu.VMEM((HEADS // 2, rows, 4 * rows), BF16),
            pltpu.VMEM((rows, 3 * INNER), BF16),
        ],
        name="time_attention",
        compiler_params=PARAMS,
    )(exchange(time_send, "tm"), time_qkv)
    x_first, dx_second = pl.pallas_call(
        last_kernel,
        out_shape=(shape_of(rows, width), shape_of(rows, width)),
        name="last",
        compiler_params=PARAMS,
    )(exchange(time_rows, "tm"), y_first, normal_second, std_second, grad_second, time_out)
    return tuple(a.reshape(shape) for a in (x_first, x_second, dx_first, dx_second))


def solution(mesh):
    in_specs = (
        P(None, "tm", "space", None),
        P(None, "tm", "space", None),
        P(None, "tm", "space", None),
        P(None, "tm", "space", None),
        P("tm", None),
        P(),
        P(),
        P(),
        P(),
    )
    out_specs = (
        P(None, "tm", "space", None),
        P(None, "tm", "space", None),
        P(None, "tm", "space", None),
        P(None, "tm", "space", None),
    )
    return jax.shard_map(
        per_device, mesh=mesh, in_specs=in_specs, out_specs=out_specs, check_vma=False
    )
```

```python
import jax
import jax.numpy as jnp
from jax import lax
from jax.experimental import pallas as pl
from jax.experimental.pallas import tpu as pltpu
from jax.sharding import PartitionSpec as P

HEADS = 8
HEAD_DIM = 64
INNER = HEADS * HEAD_DIM
EPSILON = 1e-05
FACTOR = HEAD_DIM ** (-0.5)
BF16 = jnp.bfloat16
F32 = jnp.float32
PARAMS = pltpu.CompilerParams(vmem_limit_bytes=24 << 20)


def normed(rows):
    values_f = rows.astype(F32)
    center = values_f - jnp.mean(values_f, -1, keepdims=True)
    inv_std = lax.rsqrt(jnp.mean(center * center, -1, keepdims=True) + EPSILON)
    return (center * inv_std, inv_std)


def norm_back(normal_rows, inv_std, grad_in):
    return inv_std * (
        grad_in
        - jnp.mean(grad_in, -1, keepdims=True)
        - normal_rows * jnp.mean(grad_in * normal_rows, -1, keepdims=True)
    )


def mm(left, right):
    return jnp.dot(left, right, preferred_element_type=F32)


def mm_nt(left, right):
    return lax.dot_general(left, right, (((1,), (1,)), ((), ())), preferred_element_type=F32)


def mm_tn(left, right):
    return lax.dot_general(left, right, (((0,), (0,)), ((), ())), preferred_element_type=F32)


def low_lanes(shape):
    return lax.broadcasted_iota(jnp.int32, shape, len(shape) - 1) < HEAD_DIM


def split_halves(pair, low):
    zero = jnp.zeros_like(pair)
    return (jnp.where(low, pair, zero), jnp.where(low, zero, pair))


def softmax_grads(scores, weight_grad):
    top = jnp.max(scores, 0, keepdims=True)
    powers = jnp.exp(scores - top)
    weights = powers * (1.0 / jnp.sum(powers, 0, keepdims=True))
    row_delta = jnp.sum(weights * weight_grad, 0, keepdims=True)
    score_grad = (weights * (weight_grad - row_delta)).astype(BF16)
    return (weights.astype(BF16), score_grad)


def project_kernel(
    y_hbm,
    grad_hbm,
    qkv_hbm,
    out_w_hbm,
    send_ref,
    qkv_ref,
    out_w_ref,
    normal_ref,
    std_ref,
    y_ref,
    grad_ref,
    sems,
):
    clips = send_ref.shape[0] // HEADS
    patches = send_ref.shape[1]
    pairs = [(y_hbm, y_ref), (grad_hbm, grad_ref), (out_w_hbm, out_w_ref)]
    for i in range(3):
        cols = pl.ds(INNER * i, INNER)
        pairs.append((qkv_hbm.at[:, cols], qkv_ref.at[:, cols]))
    copies = [
        pltpu.make_async_copy(source, target, sems.at[i])
        for i, (source, target) in enumerate(pairs)
    ]
    for copy in copies:
        copy.start()
    copies[0].wait()
    normal, inv_std = normed(y_ref[...])
    normal_ref[...] = normal
    std_ref[...] = jnp.broadcast_to(inv_std, std_ref.shape)
    normal = normal.astype(BF16)
    copies[1].wait()
    copies[2].wait()
    out_grad = mm_nt(grad_ref[...], out_w_ref[...])
    low = low_lanes((clips * patches, 2 * HEAD_DIM))

    def assemble(lefts, rights, part):
        for pair in range(HEADS // 2):
            cols = slice(2 * HEAD_DIM * pair, 2 * HEAD_DIM * (pair + 1))
            left, right = lefts[:, cols], rights[:, cols]
            tiles = (
                jnp.where(low, left, pltpu.roll(right, HEAD_DIM, 1)),
                jnp.where(low, pltpu.roll(left, HEAD_DIM, 1), right),
            )
            for half in range(2):
                tile = tiles[half].astype(BF16)
                for clip in range(clips):
                    send_ref[clip * HEADS + 2 * pair + half, :, 128 * part : 128 * (part + 1)] = (
                        tile[patches * clip : patches * (clip + 1)]
                    )

    def projected(i):
        copies[3 + i].wait()
        return mm(normal, qkv_ref[:, INNER * i : INNER * (i + 1)])

    assemble(projected(0), out_grad, 0)
    keys = projected(1)
    assemble(keys, projected(2), 1)


def space_kernel(pattern_ref, x_ref, out_ref, both_ref, grads_ref, own_ref, beside_ref):
    width = 2 * HEAD_DIM
    blocks = pattern_ref.shape[1]
    block = x_ref.shape[0] // blocks
    low_q = low_lanes((block, width))
    low_k = low_lanes((2 * block, width))
    scale = jnp.where(low_q, jnp.float32(FACTOR), jnp.float32(1.0))

    def rows_of(b):
        return slice(block * b, block * (b + 1))

    def stacked_queries(b):
        return jnp.concatenate(split_halves(x_ref[rows_of(b), :width], low_q), 0)

    def key_rows(b):
        beside = pl.ds(pl.multiple_of(pattern_ref[0, b] * block, block), block)
        return jnp.concatenate([x_ref[rows_of(b), width:], x_ref[beside, width:]], 0)

    def score(b):
        both_ref[b] = mm_nt(key_rows(b), stacked_queries(b))

    def weigh(b):
        weights, score_grad = softmax_grads(both_ref[b, :, :block] * FACTOR, both_ref[b, :, block:])
        grads_ref[b, :, :block] = score_grad
        grads_ref[b, :, block:] = weights

    def spread(b):
        k_low, v_high = split_halves(key_rows(b), low_k)
        rows_out = mm_tn(grads_ref[b, :, :block], k_low) + mm_tn(grads_ref[b, :, block:], v_high)
        out_ref[rows_of(b), :width] = (rows_out * scale).astype(BF16)
        key_out = mm(grads_ref[b], stacked_queries(b))
        own_ref[rows_of(b), :] = key_out[:block]
        beside_ref[rows_of(b), :] = key_out[block:]

    for step in range(blocks + 2):
        for stage, lag in ((score, 0), (weigh, 1), (spread, 2)):
            if 0 <= step - lag < blocks:
                stage(step - lag)
    for b in range(blocks):
        total = own_ref[rows_of(b), :]
        for other in range(max(b - 1, 0), min(b + 2, blocks)):
            part = beside_ref[rows_of(other), :]
            total = total + jnp.where(pattern_ref[0, other] == b, part, 0.0)
        out_ref[rows_of(b), width:] = (total * scale).astype(BF16)


def middle_kernel(
    recv_ref,
    normal_first_ref,
    std_first_ref,
    y_second_ref,
    grad_first_ref,
    space_qkv_ref,
    space_out_ref,
    time_out_ref,
    x_second_ref,
    dx_first_ref,
    send_ref,
    normal_ref,
    std_ref,
):
    clips = recv_ref.shape[0] // HEADS
    patches = recv_ref.shape[1]
    low = low_lanes((patches, 2 * HEAD_DIM))
    sections = [[], [], [], []]
    for pair in range(HEADS // 2):
        made = [[], [], [], []]
        for clip in range(clips):
            at = clip * HEADS + 2 * pair
            for i in range(2):
                first = recv_ref[at, :, 128 * i : 128 * (i + 1)].astype(F32)
                second = recv_ref[at + 1, :, 128 * i : 128 * (i + 1)].astype(F32)
                made[2 * i].append(jnp.where(low, first, pltpu.roll(second, HEAD_DIM, 1)))
                made[2 * i + 1].append(jnp.where(low, pltpu.roll(first, HEAD_DIM, 1), second))
        for i in range(4):
            sections[i].append(jnp.concatenate(made[i], 0).astype(BF16))
    query_grad, mixed, key_grad, value_grad = [jnp.concatenate(s, 1) for s in sections]
    x_second = (y_second_ref[...].astype(F32) - mm(mixed, space_out_ref[...])).astype(BF16)
    x_second_ref[...] = x_second
    normal, inv_std = normed(x_second)
    normal_ref[...] = normal
    std_ref[...] = jnp.broadcast_to(inv_std, std_ref.shape)
    dqkv = jnp.concatenate([query_grad, key_grad, value_grad], 1)
    grad_in = mm_nt(dqkv, space_qkv_ref[...])
    grad_in = norm_back(normal_first_ref[...], std_first_ref[:, :1], grad_in)
    dx_first = (grad_first_ref[...].astype(F32) + grad_in).astype(BF16)
    dx_first_ref[...] = dx_first
    time_grad = mm_nt(dx_first, time_out_ref[...]).astype(BF16)
    send_rows = jnp.concatenate([normal.astype(BF16), time_grad], 1)
    send_ref[...] = send_rows.reshape(send_ref.shape)


def time_kernel(
    x_ref,
    qkv_ref,
    x_second_ref,
    dx_first_ref,
    send_ref,
    x_second_hbm,
    dx_first_hbm,
    flat_ref,
    proj_ref,
    both_ref,
    grads_ref,
    dqkv_ref,
    sems,
):
    copies = [
        pltpu.make_async_copy(x_second_ref, x_second_hbm, sems.at[0]),
        pltpu.make_async_copy(dx_first_ref, dx_first_hbm, sems.at[1]),
    ]
    for copy in copies:
        copy.start()
    rows = x_ref.shape[0] * x_ref.shape[1]
    width = x_ref.shape[2] - INNER
    flat_ref[...] = x_ref[...].reshape(rows, width + INNER)
    for i in range(3):
        cols = slice(INNER * i, INNER * (i + 1))
        proj_ref[:, cols] = mm(flat_ref[:, :width], qkv_ref[:, cols]).astype(BF16)
    lanes = 2 * HEAD_DIM
    low = low_lanes((rows, lanes))
    row_id = lax.broadcasted_iota(jnp.int32, (rows, 2 * rows), 0)
    col_id = lax.broadcasted_iota(jnp.int32, (rows, 2 * rows), 1)
    same = ((row_id ^ col_id) & (x_ref.shape[1] - 1)) == 0
    lowest = jnp.finfo(jnp.float32).min
    pairs = HEADS // 2
    mixed_parts = []

    def split_rows(ref, start, pair):
        at = start + lanes * pair
        return jnp.concatenate(split_halves(ref[:, at : at + lanes], low), 0)

    def score(pair):
        at = lanes * pair
        keys = proj_ref[:, INNER + at : INNER + at + lanes]
        values = proj_ref[:, 2 * INNER + at : 2 * INNER + at + lanes]
        both_ref[pair, :, : 2 * rows] = mm_nt(keys, split_rows(proj_ref, 0, pair))
        both_ref[pair, :, 2 * rows :] = mm_nt(values, split_rows(flat_ref, width, pair))

    def weigh(pair):
        scores = jnp.where(same, both_ref[pair, :, : 2 * rows] * FACTOR, lowest)
        weights, score_grad = softmax_grads(scores, both_ref[pair, :, 2 * rows :])
        grads_ref[pair, :, : 2 * rows] = score_grad
        grads_ref[pair, :, 2 * rows :] = weights

    def spread(pair):
        at = lanes * pair
        score_grad = grads_ref[pair, :, : 2 * rows]
        weights = grads_ref[pair, :, 2 * rows :]
        mixed = mm_tn(
            jnp.concatenate([weights[:, :rows], weights[:, rows:]], 0),
            split_rows(proj_ref, 2 * INNER, pair),
        )
        mixed_parts.append(mixed.astype(BF16))
        query_grad = mm_tn(
            jnp.concatenate([score_grad[:, :rows], score_grad[:, rows:]], 0),
            split_rows(proj_ref, INNER, pair),
        )
        key_grad = mm(score_grad, split_rows(proj_ref, 0, pair))
        value_grad = mm(weights, split_rows(flat_ref, width, pair))
        dqkv_ref[:, at : at + lanes] = (query_grad * FACTOR).astype(BF16)
        dqkv_ref[:, INNER + at : INNER + at + lanes] = (key_grad * FACTOR).astype(BF16)
        dqkv_ref[:, 2 * INNER + at : 2 * INNER + at + lanes] = value_grad.astype(BF16)

    for step in range(pairs + 2):
        for stage, lag in ((score, 0), (weigh, 1), (spread, 2)):
            if 0 <= step - lag < pairs:
                stage(step - lag)
    grad_in = mm_nt(dqkv_ref[...], qkv_ref[...]).astype(BF16)
    send_ref[...] = jnp.concatenate(mixed_parts + [grad_in], 1).reshape(send_ref.shape)
    for copy in copies:
        copy.wait()


def last_kernel(
    recv_ref,
    y_first_ref,
    normal_ref,
    std_ref,
    grad_second_ref,
    out_w_ref,
    x_first_hbm,
    dx_hbm,
    flat_ref,
    x_first_ref,
    dx_ref,
    sems,
):
    rows = y_first_ref.shape[0]
    flat_ref[...] = recv_ref[...].reshape(flat_ref.shape)
    value = mm(flat_ref[:, :INNER], out_w_ref[...])
    x_first_ref[...] = (y_first_ref[...].astype(F32) - value).astype(BF16)
    copies = [pltpu.make_async_copy(x_first_ref, x_first_hbm, sems.at[0])]
    copies[0].start()
    parts = 2
    for i in range(parts):
        part = slice(rows // parts * i, rows // parts * (i + 1))
        grad_in = norm_back(
            normal_ref[part, :], std_ref[part, :1], flat_ref[part, INNER:].astype(F32)
        )
        dx_ref[part, :] = (grad_second_ref[part, :].astype(F32) + grad_in).astype(BF16)
        copies.append(
            pltpu.make_async_copy(dx_ref.at[part, :], dx_hbm.at[part, :], sems.at[1 + i])
        )
        copies[-1].start()
    for copy in copies:
        copy.wait()


def shape_of(*sizes):
    return jax.ShapeDtypeStruct(sizes, BF16)


def exchange(rows, axis):
    return lax.all_to_all(rows, axis, split_axis=0, concat_axis=0, tiled=True)


def per_device(
    y_first, y_second, grad_first, grad_second, pattern, time_qkv, time_out, space_qkv, space_out
):
    shape = y_first.shape
    clips, unused, patches, width = shape
    rows = clips * patches
    flat = [a.reshape(rows, width) for a in (y_first, y_second, grad_first, grad_second)]
    y_first, y_second, grad_first, grad_second = flat
    groups = clips * HEADS
    head_cols = 4 * HEAD_DIM
    blocks = pattern.shape[1]
    block = groups * patches // blocks
    frames = lax.axis_size("tm")
    wire = (frames, rows // frames, width + INNER)

    hbm = pl.BlockSpec(memory_space=pltpu.HBM)
    norm_shapes = (
        jax.ShapeDtypeStruct((rows, width), F32),
        jax.ShapeDtypeStruct((rows, 128), F32),
    )
    sent, space_qkv, space_out, normal_first, std_first = pl.pallas_call(
        project_kernel,
        out_shape=(
            shape_of(groups, patches, head_cols),
            shape_of(*space_qkv.shape),
            shape_of(*space_out.shape),
            *norm_shapes,
        ),
        in_specs=[hbm] * 4,
        scratch_shapes=[
            pltpu.VMEM((rows, width), BF16),
            pltpu.VMEM((rows, width), BF16),
            pltpu.SemaphoreType.DMA((6,)),
        ],
        name="project",
        compiler_params=PARAMS,
    )(
        *[
            pltpu.with_memory_space_constraint(a, pltpu.HBM)
            for a in (y_first, grad_second, space_qkv, space_out)
        ]
    )
    gathered = exchange(sent, "space").reshape(groups * patches, head_cols)
    space_rows = pl.pallas_call(
        space_kernel,
        out_shape=shape_of(groups * patches, head_cols),
        in_specs=[
            pl.BlockSpec(memory_space=pltpu.SMEM),
            pl.BlockSpec(memory_space=pltpu.VMEM),
        ],
        scratch_shapes=[
            pltpu.VMEM((blocks, 2 * block, 2 * block), F32),
            pltpu.VMEM((blocks, 2 * block, 2 * block), BF16),
            pltpu.VMEM((groups * patches, 2 * HEAD_DIM), F32),
            pltpu.VMEM((groups * patches, 2 * HEAD_DIM), F32),
        ],
        name="space_attention",
        compiler_params=PARAMS,
    )(pattern, gathered)
    returned = exchange(space_rows.reshape(groups, patches, head_cols), "space")
    x_second, dx_first, time_send, normal_second, std_second = pl.pallas_call(
        middle_kernel,
        out_shape=(
            pltpu.VMEM((rows, width), BF16),
            pltpu.VMEM((rows, width), BF16),
            shape_of(*wire),
            *norm_shapes,
        ),
        name="middle",
        compiler_params=PARAMS,
    )(returned, normal_first, std_first, y_second, grad_first, space_qkv, space_out, time_out)
    vmem = pl.BlockSpec(memory_space=pltpu.VMEM)
    time_rows, x_second, dx_first = pl.pallas_call(
        time_kernel,
        out_shape=(
            shape_of(*wire),
            pltpu.HBM((rows, width), BF16),
            pltpu.HBM((rows, width), BF16),
        ),
        out_specs=(vmem, hbm, hbm),
        scratch_shapes=[
            pltpu.VMEM((rows, width + INNER), BF16),
            pltpu.VMEM((rows, 3 * INNER), BF16),
            pltpu.VMEM((HEADS // 2, rows, 4 * rows), F32),
            pltpu.VMEM((HEADS // 2, rows, 4 * rows), BF16),
            pltpu.VMEM((rows, 3 * INNER), BF16),
            pltpu.SemaphoreType.DMA((2,)),
        ],
        name="time_attention",
        compiler_params=PARAMS,
    )(exchange(time_send, "tm"), time_qkv, x_second, dx_first)
    x_first, dx_second = pl.pallas_call(
        last_kernel,
        out_shape=(pltpu.HBM((rows, width), BF16), pltpu.HBM((rows, width), BF16)),
        out_specs=(hbm, hbm),
        scratch_shapes=[
            pltpu.VMEM((rows, width + INNER), BF16),
            pltpu.VMEM((rows, width), BF16),
            pltpu.VMEM((rows, width), BF16),
            pltpu.SemaphoreType.DMA((3,)),
        ],
        name="last",
        compiler_params=PARAMS,
    )(exchange(time_rows, "tm"), y_first, normal_second, std_second, grad_second, time_out)
    return tuple(a.reshape(shape) for a in (x_first, x_second, dx_first, dx_second))


def solution(mesh):
    in_specs = (
        P(None, "tm", "space", None),
        P(None, "tm", "space", None),
        P(None, "tm", "space", None),
        P(None, "tm", "space", None),
        P("tm", None),
        P(),
        P(),
        P(),
        P(),
    )
    out_specs = (
        P(None, "tm", "space", None),
        P(None, "tm", "space", None),
        P(None, "tm", "space", None),
        P(None, "tm", "space", None),
    )
    return jax.shard_map(
        per_device, mesh=mesh, in_specs=in_specs, out_specs=out_specs, check_vma=False
    )
```

```python
import jax
import jax.numpy as jnp
from jax import lax
from jax.experimental import pallas as pl
from jax.experimental.pallas import tpu as pltpu
from jax.sharding import PartitionSpec as P

HEADS = 8
HEAD_DIM = 64
INNER = HEADS * HEAD_DIM
EPSILON = 1e-05
FACTOR = HEAD_DIM ** (-0.5)
BF16 = jnp.bfloat16
F32 = jnp.float32
PARAMS = pltpu.CompilerParams(vmem_limit_bytes=24 << 20)


def normed(rows):
    values_f = rows.astype(F32)
    center = values_f - jnp.mean(values_f, -1, keepdims=True)
    inv_std = lax.rsqrt(jnp.mean(center * center, -1, keepdims=True) + EPSILON)
    return (center * inv_std, inv_std)


def norm_back(normal_rows, inv_std, grad_in):
    return inv_std * (
        grad_in
        - jnp.mean(grad_in, -1, keepdims=True)
        - normal_rows * jnp.mean(grad_in * normal_rows, -1, keepdims=True)
    )


def mm(left, right):
    return jnp.dot(left, right, preferred_element_type=F32)


def mm_nt(left, right):
    return lax.dot_general(left, right, (((1,), (1,)), ((), ())), preferred_element_type=F32)


def mm_tn(left, right):
    return lax.dot_general(left, right, (((0,), (0,)), ((), ())), preferred_element_type=F32)


def low_lanes(shape):
    return lax.broadcasted_iota(jnp.int32, shape, len(shape) - 1) < HEAD_DIM


def split_halves(pair, low):
    zero = jnp.zeros_like(pair)
    return (jnp.where(low, pair, zero), jnp.where(low, zero, pair))


def softmax_grads(scores, weight_grad):
    top = jnp.max(scores, 0, keepdims=True)
    powers = jnp.exp(scores - top)
    weights = powers * (1.0 / jnp.sum(powers, 0, keepdims=True))
    row_delta = jnp.sum(weights * weight_grad, 0, keepdims=True)
    score_grad = (weights * (weight_grad - row_delta)).astype(BF16)
    return (weights.astype(BF16), score_grad)


def project_kernel(
    y_hbm,
    grad_hbm,
    qkv_hbm,
    out_w_hbm,
    send_ref,
    qkv_ref,
    out_w_ref,
    normal_ref,
    std_ref,
    y_ref,
    grad_ref,
    sems,
):
    clips = send_ref.shape[0] // HEADS
    patches = send_ref.shape[1]
    pairs = [(y_hbm, y_ref), (grad_hbm, grad_ref), (out_w_hbm, out_w_ref)]
    for i in range(3):
        cols = pl.ds(INNER * i, INNER)
        pairs.append((qkv_hbm.at[:, cols], qkv_ref.at[:, cols]))
    copies = [
        pltpu.make_async_copy(source, target, sems.at[i])
        for i, (source, target) in enumerate(pairs)
    ]
    for copy in copies:
        copy.start()
    copies[0].wait()
    normal, inv_std = normed(y_ref[...])
    normal_ref[...] = normal
    std_ref[...] = jnp.broadcast_to(inv_std, std_ref.shape)
    normal = normal.astype(BF16)
    copies[1].wait()
    copies[2].wait()
    out_grad = mm_nt(grad_ref[...], out_w_ref[...])
    low = low_lanes((clips * patches, 2 * HEAD_DIM))

    def assemble(lefts, rights, part):
        for pair in range(HEADS // 2):
            cols = slice(2 * HEAD_DIM * pair, 2 * HEAD_DIM * (pair + 1))
            left, right = lefts[:, cols], rights[:, cols]
            tiles = (
                jnp.where(low, left, pltpu.roll(right, HEAD_DIM, 1)),
                jnp.where(low, pltpu.roll(left, HEAD_DIM, 1), right),
            )
            for half in range(2):
                tile = tiles[half].astype(BF16)
                for clip in range(clips):
                    send_ref[clip * HEADS + 2 * pair + half, :, 128 * part : 128 * (part + 1)] = (
                        tile[patches * clip : patches * (clip + 1)]
                    )

    def projected(i):
        copies[3 + i].wait()
        return mm(normal, qkv_ref[:, INNER * i : INNER * (i + 1)])

    assemble(projected(0), out_grad, 0)
    keys = projected(1)
    assemble(keys, projected(2), 1)


def space_kernel(
    pattern_ref,
    x_ref,
    y_second_hbm,
    grad_first_hbm,
    time_out_hbm,
    out_ref,
    y_second_ref,
    grad_first_ref,
    time_out_ref,
    both_ref,
    grads_ref,
    own_ref,
    beside_ref,
    sems,
):
    copies = [
        pltpu.make_async_copy(y_second_hbm, y_second_ref, sems.at[0]),
        pltpu.make_async_copy(grad_first_hbm, grad_first_ref, sems.at[1]),
        pltpu.make_async_copy(time_out_hbm, time_out_ref, sems.at[2]),
    ]
    for copy in copies:
        copy.start()
    width = 2 * HEAD_DIM
    blocks = pattern_ref.shape[1]
    block = x_ref.shape[0] // blocks
    low_q = low_lanes((block, width))
    low_k = low_lanes((2 * block, width))
    scale = jnp.where(low_q, jnp.float32(FACTOR), jnp.float32(1.0))

    def rows_of(b):
        return slice(block * b, block * (b + 1))

    def stacked_queries(b):
        return jnp.concatenate(split_halves(x_ref[rows_of(b), :width], low_q), 0)

    def key_rows(b):
        beside = pl.ds(pl.multiple_of(pattern_ref[0, b] * block, block), block)
        return jnp.concatenate([x_ref[rows_of(b), width:], x_ref[beside, width:]], 0)

    def score(b):
        both_ref[b] = mm_nt(key_rows(b), stacked_queries(b))

    def weigh(b):
        weights, score_grad = softmax_grads(both_ref[b, :, :block] * FACTOR, both_ref[b, :, block:])
        grads_ref[b, :, :block] = score_grad
        grads_ref[b, :, block:] = weights

    def spread(b):
        k_low, v_high = split_halves(key_rows(b), low_k)
        rows_out = mm_tn(grads_ref[b, :, :block], k_low) + mm_tn(grads_ref[b, :, block:], v_high)
        out_ref[rows_of(b), :width] = (rows_out * scale).astype(BF16)
        key_out = mm(grads_ref[b], stacked_queries(b))
        own_ref[rows_of(b), :] = key_out[:block]
        beside_ref[rows_of(b), :] = key_out[block:]

    for step in range(blocks + 3):
        for stage, lag in ((score, 0), (weigh, 2), (spread, 3)):
            if 0 <= step - lag < blocks:
                stage(step - lag)
    for b in range(blocks):
        total = own_ref[rows_of(b), :]
        for other in range(max(b - 1, 0), min(b + 2, blocks)):
            part = beside_ref[rows_of(other), :]
            total = total + jnp.where(pattern_ref[0, other] == b, part, 0.0)
        out_ref[rows_of(b), width:] = (total * scale).astype(BF16)
    for copy in copies:
        copy.wait()


def middle_kernel(
    recv_ref,
    normal_first_ref,
    std_first_ref,
    y_second_ref,
    grad_first_ref,
    space_qkv_ref,
    space_out_ref,
    time_out_ref,
    x_second_ref,
    dx_first_ref,
    send_ref,
    normal_ref,
    std_ref,
):
    clips = recv_ref.shape[0] // HEADS
    patches = recv_ref.shape[1]
    low = low_lanes((patches, 2 * HEAD_DIM))
    sections = [[], [], [], []]
    for pair in range(HEADS // 2):
        made = [[], [], [], []]
        for clip in range(clips):
            at = clip * HEADS + 2 * pair
            for i in range(2):
                first = recv_ref[at, :, 128 * i : 128 * (i + 1)].astype(F32)
                second = recv_ref[at + 1, :, 128 * i : 128 * (i + 1)].astype(F32)
                made[2 * i].append(jnp.where(low, first, pltpu.roll(second, HEAD_DIM, 1)))
                made[2 * i + 1].append(jnp.where(low, pltpu.roll(first, HEAD_DIM, 1), second))
        for i in range(4):
            sections[i].append(jnp.concatenate(made[i], 0).astype(BF16))
    query_grad, mixed, key_grad, value_grad = [jnp.concatenate(s, 1) for s in sections]
    x_second = (y_second_ref[...].astype(F32) - mm(mixed, space_out_ref[...])).astype(BF16)
    x_second_ref[...] = x_second
    normal, inv_std = normed(x_second)
    normal_ref[...] = normal
    std_ref[...] = jnp.broadcast_to(inv_std, std_ref.shape)
    dqkv = jnp.concatenate([query_grad, key_grad, value_grad], 1)
    grad_in = mm_nt(dqkv, space_qkv_ref[...])
    grad_in = norm_back(normal_first_ref[...], std_first_ref[:, :1], grad_in)
    dx_first = (grad_first_ref[...].astype(F32) + grad_in).astype(BF16)
    dx_first_ref[...] = dx_first
    time_grad = mm_nt(dx_first, time_out_ref[...]).astype(BF16)
    send_rows = jnp.concatenate([normal.astype(BF16), time_grad], 1)
    send_ref[...] = send_rows.reshape(send_ref.shape)


def time_kernel(
    x_ref,
    qkv_ref,
    x_second_ref,
    dx_first_ref,
    send_ref,
    x_second_hbm,
    dx_first_hbm,
    flat_ref,
    proj_ref,
    both_ref,
    grads_ref,
    dqkv_ref,
    sems,
):
    copies = [
        pltpu.make_async_copy(x_second_ref, x_second_hbm, sems.at[0]),
        pltpu.make_async_copy(dx_first_ref, dx_first_hbm, sems.at[1]),
    ]
    for copy in copies:
        copy.start()
    rows = x_ref.shape[0] * x_ref.shape[1]
    width = x_ref.shape[2] - INNER
    flat_ref[...] = x_ref[...].reshape(rows, width + INNER)
    for i in range(3):
        cols = slice(INNER * i, INNER * (i + 1))
        proj_ref[:, cols] = mm(flat_ref[:, :width], qkv_ref[:, cols]).astype(BF16)
    lanes = 2 * HEAD_DIM
    low = low_lanes((rows, lanes))
    row_id = lax.broadcasted_iota(jnp.int32, (rows, 2 * rows), 0)
    col_id = lax.broadcasted_iota(jnp.int32, (rows, 2 * rows), 1)
    same = ((row_id ^ col_id) & (x_ref.shape[1] - 1)) == 0
    lowest = jnp.finfo(jnp.float32).min
    pairs = HEADS // 2
    mixed_parts = []

    def split_rows(ref, start, pair):
        at = start + lanes * pair
        return jnp.concatenate(split_halves(ref[:, at : at + lanes], low), 0)

    def score(pair):
        at = lanes * pair
        keys = proj_ref[:, INNER + at : INNER + at + lanes]
        values = proj_ref[:, 2 * INNER + at : 2 * INNER + at + lanes]
        both_ref[pair, :, : 2 * rows] = mm_nt(keys, split_rows(proj_ref, 0, pair))
        both_ref[pair, :, 2 * rows :] = mm_nt(values, split_rows(flat_ref, width, pair))

    def weigh(pair):
        scores = jnp.where(same, both_ref[pair, :, : 2 * rows] * FACTOR, lowest)
        weights, score_grad = softmax_grads(scores, both_ref[pair, :, 2 * rows :])
        grads_ref[pair, :, : 2 * rows] = score_grad
        grads_ref[pair, :, 2 * rows :] = weights

    def spread(pair):
        at = lanes * pair
        score_grad = grads_ref[pair, :, : 2 * rows]
        weights = grads_ref[pair, :, 2 * rows :]
        mixed = mm_tn(
            jnp.concatenate([weights[:, :rows], weights[:, rows:]], 0),
            split_rows(proj_ref, 2 * INNER, pair),
        )
        mixed_parts.append(mixed.astype(BF16))
        query_grad = mm_tn(
            jnp.concatenate([score_grad[:, :rows], score_grad[:, rows:]], 0),
            split_rows(proj_ref, INNER, pair),
        )
        key_grad = mm(score_grad, split_rows(proj_ref, 0, pair))
        value_grad = mm(weights, split_rows(flat_ref, width, pair))
        dqkv_ref[:, at : at + lanes] = (query_grad * FACTOR).astype(BF16)
        dqkv_ref[:, INNER + at : INNER + at + lanes] = (key_grad * FACTOR).astype(BF16)
        dqkv_ref[:, 2 * INNER + at : 2 * INNER + at + lanes] = value_grad.astype(BF16)

    for step in range(pairs + 2):
        for stage, lag in ((score, 0), (weigh, 1), (spread, 2)):
            if 0 <= step - lag < pairs:
                stage(step - lag)
    grad_in = mm_nt(dqkv_ref[...], qkv_ref[...]).astype(BF16)
    send_ref[...] = jnp.concatenate(mixed_parts + [grad_in], 1).reshape(send_ref.shape)
    for copy in copies:
        copy.wait()


def last_kernel(
    recv_ref,
    y_first_ref,
    normal_ref,
    std_ref,
    grad_second_ref,
    out_w_ref,
    x_first_hbm,
    dx_hbm,
    flat_ref,
    x_first_ref,
    dx_ref,
    sems,
):
    rows = y_first_ref.shape[0]
    flat_ref[...] = recv_ref[...].reshape(flat_ref.shape)
    value = mm(flat_ref[:, :INNER], out_w_ref[...])
    x_first_ref[...] = (y_first_ref[...].astype(F32) - value).astype(BF16)
    copies = [pltpu.make_async_copy(x_first_ref, x_first_hbm, sems.at[0])]
    copies[0].start()
    parts = 2
    for i in range(parts):
        part = slice(rows // parts * i, rows // parts * (i + 1))
        grad_in = norm_back(
            normal_ref[part, :], std_ref[part, :1], flat_ref[part, INNER:].astype(F32)
        )
        dx_ref[part, :] = (grad_second_ref[part, :].astype(F32) + grad_in).astype(BF16)
        copies.append(
            pltpu.make_async_copy(dx_ref.at[part, :], dx_hbm.at[part, :], sems.at[1 + i])
        )
        copies[-1].start()
    for copy in copies:
        copy.wait()


def shape_of(*sizes):
    return jax.ShapeDtypeStruct(sizes, BF16)


def exchange(rows, axis):
    return lax.all_to_all(rows, axis, split_axis=0, concat_axis=0, tiled=True)


def per_device(
    y_first, y_second, grad_first, grad_second, pattern, time_qkv, time_out, space_qkv, space_out
):
    shape = y_first.shape
    clips, unused, patches, width = shape
    rows = clips * patches
    flat = [a.reshape(rows, width) for a in (y_first, y_second, grad_first, grad_second)]
    y_first, y_second, grad_first, grad_second = flat
    groups = clips * HEADS
    head_cols = 4 * HEAD_DIM
    blocks = pattern.shape[1]
    block = groups * patches // blocks
    frames = lax.axis_size("tm")
    wire = (frames, rows // frames, width + INNER)

    hbm = pl.BlockSpec(memory_space=pltpu.HBM)
    vmem = pl.BlockSpec(memory_space=pltpu.VMEM)
    norm_shapes = (
        jax.ShapeDtypeStruct((rows, width), F32),
        jax.ShapeDtypeStruct((rows, 128), F32),
    )
    sent, space_qkv, space_out, normal_first, std_first = pl.pallas_call(
        project_kernel,
        out_shape=(
            shape_of(groups, patches, head_cols),
            shape_of(*space_qkv.shape),
            shape_of(*space_out.shape),
            *norm_shapes,
        ),
        in_specs=[hbm] * 4,
        scratch_shapes=[
            pltpu.VMEM((rows, width), BF16),
            pltpu.VMEM((rows, width), BF16),
            pltpu.SemaphoreType.DMA((6,)),
        ],
        name="project",
        compiler_params=PARAMS,
    )(
        *[
            pltpu.with_memory_space_constraint(a, pltpu.HBM)
            for a in (y_first, grad_second, space_qkv, space_out)
        ]
    )
    gathered = exchange(sent, "space").reshape(groups * patches, head_cols)
    space_rows, y_second, grad_first, time_out = pl.pallas_call(
        space_kernel,
        out_shape=(
            shape_of(groups * patches, head_cols),
            pltpu.VMEM((rows, width), BF16),
            pltpu.VMEM((rows, width), BF16),
            pltpu.VMEM(time_out.shape, BF16),
        ),
        in_specs=[pl.BlockSpec(memory_space=pltpu.SMEM), vmem, hbm, hbm, hbm],
        scratch_shapes=[
            pltpu.VMEM((blocks, 2 * block, 2 * block), F32),
            pltpu.VMEM((blocks, 2 * block, 2 * block), BF16),
            pltpu.VMEM((groups * patches, 2 * HEAD_DIM), F32),
            pltpu.VMEM((groups * patches, 2 * HEAD_DIM), F32),
            pltpu.SemaphoreType.DMA((3,)),
        ],
        name="space_attention",
        compiler_params=PARAMS,
    )(
        pattern,
        gathered,
        *[
            pltpu.with_memory_space_constraint(a, pltpu.HBM)
            for a in (y_second, grad_first, time_out)
        ],
    )
    returned = exchange(space_rows.reshape(groups, patches, head_cols), "space")
    x_second, dx_first, time_send, normal_second, std_second = pl.pallas_call(
        middle_kernel,
        out_shape=(
            pltpu.VMEM((rows, width), BF16),
            pltpu.VMEM((rows, width), BF16),
            shape_of(*wire),
            *norm_shapes,
        ),
        name="middle",
        compiler_params=PARAMS,
    )(returned, normal_first, std_first, y_second, grad_first, space_qkv, space_out, time_out)
    time_rows, x_second, dx_first = pl.pallas_call(
        time_kernel,
        out_shape=(
            shape_of(*wire),
            pltpu.HBM((rows, width), BF16),
            pltpu.HBM((rows, width), BF16),
        ),
        out_specs=(vmem, hbm, hbm),
        scratch_shapes=[
            pltpu.VMEM((rows, width + INNER), BF16),
            pltpu.VMEM((rows, 3 * INNER), BF16),
            pltpu.VMEM((HEADS // 2, rows, 4 * rows), F32),
            pltpu.VMEM((HEADS // 2, rows, 4 * rows), BF16),
            pltpu.VMEM((rows, 3 * INNER), BF16),
            pltpu.SemaphoreType.DMA((2,)),
        ],
        name="time_attention",
        compiler_params=PARAMS,
    )(exchange(time_send, "tm"), time_qkv, x_second, dx_first)
    x_first, dx_second = pl.pallas_call(
        last_kernel,
        out_shape=(pltpu.HBM((rows, width), BF16), pltpu.HBM((rows, width), BF16)),
        out_specs=(hbm, hbm),
        scratch_shapes=[
            pltpu.VMEM((rows, width + INNER), BF16),
            pltpu.VMEM((rows, width), BF16),
            pltpu.VMEM((rows, width), BF16),
            pltpu.SemaphoreType.DMA((3,)),
        ],
        name="last",
        compiler_params=PARAMS,
    )(exchange(time_rows, "tm"), y_first, normal_second, std_second, grad_second, time_out)
    return tuple(a.reshape(shape) for a in (x_first, x_second, dx_first, dx_second))


def solution(mesh):
    in_specs = (
        P(None, "tm", "space", None),
        P(None, "tm", "space", None),
        P(None, "tm", "space", None),
        P(None, "tm", "space", None),
        P("tm", None),
        P(),
        P(),
        P(),
        P(),
    )
    out_specs = (
        P(None, "tm", "space", None),
        P(None, "tm", "space", None),
        P(None, "tm", "space", None),
        P(None, "tm", "space", None),
    )
    return jax.shard_map(
        per_device, mesh=mesh, in_specs=in_specs, out_specs=out_specs, check_vma=False
    )
```

```python
import jax
import jax.numpy as jnp
from jax import lax
from jax.experimental import pallas as pl
from jax.experimental.pallas import tpu as pltpu
from jax.sharding import PartitionSpec as P

HEADS = 8
HEAD_DIM = 64
INNER = HEADS * HEAD_DIM
EPSILON = 1e-05
FACTOR = HEAD_DIM ** (-0.5)
BF16 = jnp.bfloat16
F32 = jnp.float32
PARAMS = pltpu.CompilerParams(vmem_limit_bytes=24 << 20)


def normed(rows):
    values_f = rows.astype(F32)
    center = values_f - jnp.mean(values_f, -1, keepdims=True)
    inv_std = lax.rsqrt(jnp.mean(center * center, -1, keepdims=True) + EPSILON)
    return (center * inv_std, inv_std)


def norm_back(normal_rows, inv_std, grad_in):
    return inv_std * (
        grad_in
        - jnp.mean(grad_in, -1, keepdims=True)
        - normal_rows * jnp.mean(grad_in * normal_rows, -1, keepdims=True)
    )


def mm(left, right):
    return jnp.dot(left, right, preferred_element_type=F32)


def mm_nt(left, right):
    return lax.dot_general(left, right, (((1,), (1,)), ((), ())), preferred_element_type=F32)


def mm_tn(left, right):
    return lax.dot_general(left, right, (((0,), (0,)), ((), ())), preferred_element_type=F32)


def low_lanes(shape):
    return lax.broadcasted_iota(jnp.int32, shape, len(shape) - 1) < HEAD_DIM


def split_halves(pair, low):
    zero = jnp.zeros_like(pair)
    return (jnp.where(low, pair, zero), jnp.where(low, zero, pair))


def softmax_grads(scores, weight_grad):
    top = jnp.max(scores, 0, keepdims=True)
    powers = jnp.exp(scores - top)
    weights = powers * (1.0 / jnp.sum(powers, 0, keepdims=True))
    row_delta = jnp.sum(weights * weight_grad, 0, keepdims=True)
    score_grad = (weights * (weight_grad - row_delta)).astype(BF16)
    return (weights.astype(BF16), score_grad)


def project_kernel(
    y_hbm,
    grad_hbm,
    qkv_hbm,
    out_w_hbm,
    send_ref,
    qkv_ref,
    out_w_ref,
    normal_ref,
    std_ref,
    y_ref,
    grad_ref,
    sems,
):
    clips = send_ref.shape[0] // HEADS
    patches = send_ref.shape[1]
    pairs = [(y_hbm, y_ref), (grad_hbm, grad_ref), (out_w_hbm, out_w_ref)]
    for i in range(3):
        cols = pl.ds(INNER * i, INNER)
        pairs.append((qkv_hbm.at[:, cols], qkv_ref.at[:, cols]))
    copies = [
        pltpu.make_async_copy(source, target, sems.at[i])
        for i, (source, target) in enumerate(pairs)
    ]
    for copy in copies:
        copy.start()
    copies[0].wait()
    normal, inv_std = normed(y_ref[...])
    normal_ref[...] = normal
    std_ref[...] = jnp.broadcast_to(inv_std, std_ref.shape)
    normal = normal.astype(BF16)
    copies[1].wait()
    copies[2].wait()
    out_grad = mm_nt(grad_ref[...], out_w_ref[...])
    low = low_lanes((clips * patches, 2 * HEAD_DIM))

    def assemble(lefts, rights, part):
        for pair in range(HEADS // 2):
            cols = slice(2 * HEAD_DIM * pair, 2 * HEAD_DIM * (pair + 1))
            left, right = lefts[:, cols], rights[:, cols]
            tiles = (
                jnp.where(low, left, pltpu.roll(right, HEAD_DIM, 1)),
                jnp.where(low, pltpu.roll(left, HEAD_DIM, 1), right),
            )
            for half in range(2):
                tile = tiles[half].astype(BF16)
                for clip in range(clips):
                    send_ref[clip * HEADS + 2 * pair + half, :, 128 * part : 128 * (part + 1)] = (
                        tile[patches * clip : patches * (clip + 1)]
                    )

    def projected(i):
        copies[3 + i].wait()
        return mm(normal, qkv_ref[:, INNER * i : INNER * (i + 1)])

    assemble(projected(0), out_grad, 0)
    keys = projected(1)
    assemble(keys, projected(2), 1)


def space_kernel(pattern_ref, x_ref, out_ref, both_ref, grads_ref, own_ref, beside_ref):
    width = 2 * HEAD_DIM
    blocks = pattern_ref.shape[1]
    block = x_ref.shape[0] // blocks
    low_q = low_lanes((block, width))
    low_k = low_lanes((2 * block, width))
    scale = jnp.where(low_q, jnp.float32(FACTOR), jnp.float32(1.0))

    def rows_of(b):
        return slice(block * b, block * (b + 1))

    def stacked_queries(b):
        return jnp.concatenate(split_halves(x_ref[rows_of(b), :width], low_q), 0)

    def key_rows(b):
        beside = pl.ds(pl.multiple_of(pattern_ref[0, b] * block, block), block)
        return jnp.concatenate([x_ref[rows_of(b), width:], x_ref[beside, width:]], 0)

    def score(b):
        both_ref[b] = mm_nt(key_rows(b), stacked_queries(b))

    def weigh(b):
        weights, score_grad = softmax_grads(both_ref[b, :, :block] * FACTOR, both_ref[b, :, block:])
        grads_ref[b, :, :block] = score_grad
        grads_ref[b, :, block:] = weights

    def spread(b):
        k_low, v_high = split_halves(key_rows(b), low_k)
        rows_out = mm_tn(grads_ref[b, :, :block], k_low) + mm_tn(grads_ref[b, :, block:], v_high)
        out_ref[rows_of(b), :width] = (rows_out * scale).astype(BF16)
        key_out = mm(grads_ref[b], stacked_queries(b))
        own_ref[rows_of(b), :] = key_out[:block]
        beside_ref[rows_of(b), :] = key_out[block:]

    for step in range(blocks + 3):
        for stage, lag in ((score, 0), (weigh, 2), (spread, 3)):
            if 0 <= step - lag < blocks:
                stage(step - lag)
    for b in range(blocks):
        total = own_ref[rows_of(b), :]
        for other in range(max(b - 1, 0), min(b + 2, blocks)):
            part = beside_ref[rows_of(other), :]
            total = total + jnp.where(pattern_ref[0, other] == b, part, 0.0)
        out_ref[rows_of(b), width:] = (total * scale).astype(BF16)


def middle_kernel(
    recv_ref,
    normal_first_ref,
    std_first_ref,
    y_second_ref,
    grad_first_ref,
    space_qkv_ref,
    space_out_ref,
    time_out_ref,
    x_second_ref,
    dx_first_ref,
    send_ref,
    normal_ref,
    std_ref,
):
    clips = recv_ref.shape[0] // HEADS
    patches = recv_ref.shape[1]
    low = low_lanes((patches, 2 * HEAD_DIM))
    sections = [[], [], [], []]
    for pair in range(HEADS // 2):
        made = [[], [], [], []]
        for clip in range(clips):
            at = clip * HEADS + 2 * pair
            for i in range(2):
                first = recv_ref[at, :, 128 * i : 128 * (i + 1)].astype(F32)
                second = recv_ref[at + 1, :, 128 * i : 128 * (i + 1)].astype(F32)
                made[2 * i].append(jnp.where(low, first, pltpu.roll(second, HEAD_DIM, 1)))
                made[2 * i + 1].append(jnp.where(low, pltpu.roll(first, HEAD_DIM, 1), second))
        for i in range(4):
            sections[i].append(jnp.concatenate(made[i], 0).astype(BF16))
    query_grad, mixed, key_grad, value_grad = [jnp.concatenate(s, 1) for s in sections]
    x_second = (y_second_ref[...].astype(F32) - mm(mixed, space_out_ref[...])).astype(BF16)
    x_second_ref[...] = x_second
    normal, inv_std = normed(x_second)
    normal_ref[...] = normal
    std_ref[...] = jnp.broadcast_to(inv_std, std_ref.shape)
    dqkv = jnp.concatenate([query_grad, key_grad, value_grad], 1)
    grad_in = mm_nt(dqkv, space_qkv_ref[...])
    grad_in = norm_back(normal_first_ref[...], std_first_ref[:, :1], grad_in)
    dx_first = (grad_first_ref[...].astype(F32) + grad_in).astype(BF16)
    dx_first_ref[...] = dx_first
    time_grad = mm_nt(dx_first, time_out_ref[...]).astype(BF16)
    send_rows = jnp.concatenate([normal.astype(BF16), time_grad], 1)
    send_ref[...] = send_rows.reshape(send_ref.shape)


def time_kernel(
    x_ref,
    qkv_ref,
    x_second_ref,
    dx_first_ref,
    send_ref,
    x_second_hbm,
    dx_first_hbm,
    flat_ref,
    proj_ref,
    both_ref,
    grads_ref,
    dqkv_ref,
    sems,
):
    copies = [
        pltpu.make_async_copy(x_second_ref, x_second_hbm, sems.at[0]),
        pltpu.make_async_copy(dx_first_ref, dx_first_hbm, sems.at[1]),
    ]
    for copy in copies:
        copy.start()
    rows = x_ref.shape[0] * x_ref.shape[1]
    width = x_ref.shape[2] - INNER
    flat_ref[...] = x_ref[...].reshape(rows, width + INNER)
    for i in range(3):
        cols = slice(INNER * i, INNER * (i + 1))
        proj_ref[:, cols] = mm(flat_ref[:, :width], qkv_ref[:, cols]).astype(BF16)
    lanes = 2 * HEAD_DIM
    low = low_lanes((rows, lanes))
    row_id = lax.broadcasted_iota(jnp.int32, (rows, 2 * rows), 0)
    col_id = lax.broadcasted_iota(jnp.int32, (rows, 2 * rows), 1)
    same = ((row_id ^ col_id) & (x_ref.shape[1] - 1)) == 0
    lowest = jnp.finfo(jnp.float32).min
    pairs = HEADS // 2
    mixed_parts = []

    def split_rows(ref, start, pair):
        at = start + lanes * pair
        return jnp.concatenate(split_halves(ref[:, at : at + lanes], low), 0)

    def score(pair):
        at = lanes * pair
        keys = proj_ref[:, INNER + at : INNER + at + lanes]
        values = proj_ref[:, 2 * INNER + at : 2 * INNER + at + lanes]
        both_ref[pair, :, : 2 * rows] = mm_nt(keys, split_rows(proj_ref, 0, pair))
        both_ref[pair, :, 2 * rows :] = mm_nt(values, split_rows(flat_ref, width, pair))

    def weigh(pair):
        scores = jnp.where(same, both_ref[pair, :, : 2 * rows] * FACTOR, lowest)
        weights, score_grad = softmax_grads(scores, both_ref[pair, :, 2 * rows :])
        grads_ref[pair, :, : 2 * rows] = score_grad
        grads_ref[pair, :, 2 * rows :] = weights

    def spread(pair):
        at = lanes * pair
        score_grad = grads_ref[pair, :, : 2 * rows]
        weights = grads_ref[pair, :, 2 * rows :]
        mixed = mm_tn(
            jnp.concatenate([weights[:, :rows], weights[:, rows:]], 0),
            split_rows(proj_ref, 2 * INNER, pair),
        )
        mixed_parts.append(mixed.astype(BF16))
        query_grad = mm_tn(
            jnp.concatenate([score_grad[:, :rows], score_grad[:, rows:]], 0),
            split_rows(proj_ref, INNER, pair),
        )
        key_grad = mm(score_grad, split_rows(proj_ref, 0, pair))
        value_grad = mm(weights, split_rows(flat_ref, width, pair))
        dqkv_ref[:, at : at + lanes] = (query_grad * FACTOR).astype(BF16)
        dqkv_ref[:, INNER + at : INNER + at + lanes] = (key_grad * FACTOR).astype(BF16)
        dqkv_ref[:, 2 * INNER + at : 2 * INNER + at + lanes] = value_grad.astype(BF16)

    for step in range(pairs + 2):
        for stage, lag in ((score, 0), (weigh, 1), (spread, 2)):
            if 0 <= step - lag < pairs:
                stage(step - lag)
    grad_in = mm_nt(dqkv_ref[...], qkv_ref[...]).astype(BF16)
    send_ref[...] = jnp.concatenate(mixed_parts + [grad_in], 1).reshape(send_ref.shape)
    for copy in copies:
        copy.wait()


def last_kernel(
    recv_ref,
    y_first_ref,
    normal_ref,
    std_ref,
    grad_second_ref,
    out_w_ref,
    x_first_hbm,
    dx_hbm,
    flat_ref,
    x_first_ref,
    dx_ref,
    sems,
):
    rows = y_first_ref.shape[0]
    flat_ref[...] = recv_ref[...].reshape(flat_ref.shape)
    value = mm(flat_ref[:, :INNER], out_w_ref[...])
    x_first_ref[...] = (y_first_ref[...].astype(F32) - value).astype(BF16)
    copies = [pltpu.make_async_copy(x_first_ref, x_first_hbm, sems.at[0])]
    copies[0].start()
    parts = 4
    for i in range(parts):
        part = slice(rows // parts * i, rows // parts * (i + 1))
        grad_in = norm_back(
            normal_ref[part, :], std_ref[part, :1], flat_ref[part, INNER:].astype(F32)
        )
        dx_ref[part, :] = (grad_second_ref[part, :].astype(F32) + grad_in).astype(BF16)
        copies.append(
            pltpu.make_async_copy(dx_ref.at[part, :], dx_hbm.at[part, :], sems.at[1 + i])
        )
        copies[-1].start()
    for copy in copies:
        copy.wait()


def shape_of(*sizes):
    return jax.ShapeDtypeStruct(sizes, BF16)


def exchange(rows, axis):
    return lax.all_to_all(rows, axis, split_axis=0, concat_axis=0, tiled=True)


def per_device(
    y_first, y_second, grad_first, grad_second, pattern, time_qkv, time_out, space_qkv, space_out
):
    shape = y_first.shape
    clips, unused, patches, width = shape
    rows = clips * patches
    flat = [a.reshape(rows, width) for a in (y_first, y_second, grad_first, grad_second)]
    y_first, y_second, grad_first, grad_second = flat
    groups = clips * HEADS
    head_cols = 4 * HEAD_DIM
    blocks = pattern.shape[1]
    block = groups * patches // blocks
    frames = lax.axis_size("tm")
    wire = (frames, rows // frames, width + INNER)

    hbm = pl.BlockSpec(memory_space=pltpu.HBM)
    norm_shapes = (
        jax.ShapeDtypeStruct((rows, width), F32),
        jax.ShapeDtypeStruct((rows, 128), F32),
    )
    sent, space_qkv, space_out, normal_first, std_first = pl.pallas_call(
        project_kernel,
        out_shape=(
            shape_of(groups, patches, head_cols),
            shape_of(*space_qkv.shape),
            shape_of(*space_out.shape),
            *norm_shapes,
        ),
        in_specs=[hbm] * 4,
        scratch_shapes=[
            pltpu.VMEM((rows, width), BF16),
            pltpu.VMEM((rows, width), BF16),
            pltpu.SemaphoreType.DMA((6,)),
        ],
        name="project",
        compiler_params=PARAMS,
    )(
        *[
            pltpu.with_memory_space_constraint(a, pltpu.HBM)
            for a in (y_first, grad_second, space_qkv, space_out)
        ]
    )
    gathered = exchange(sent, "space").reshape(groups * patches, head_cols)
    space_rows = pl.pallas_call(
        space_kernel,
        out_shape=shape_of(groups * patches, head_cols),
        in_specs=[
            pl.BlockSpec(memory_space=pltpu.SMEM),
            pl.BlockSpec(memory_space=pltpu.VMEM),
        ],
        scratch_shapes=[
            pltpu.VMEM((blocks, 2 * block, 2 * block), F32),
            pltpu.VMEM((blocks, 2 * block, 2 * block), BF16),
            pltpu.VMEM((groups * patches, 2 * HEAD_DIM), F32),
            pltpu.VMEM((groups * patches, 2 * HEAD_DIM), F32),
        ],
        name="space_attention",
        compiler_params=PARAMS,
    )(pattern, gathered)
    returned = exchange(space_rows.reshape(groups, patches, head_cols), "space")
    x_second, dx_first, time_send, normal_second, std_second = pl.pallas_call(
        middle_kernel,
        out_shape=(
            pltpu.VMEM((rows, width), BF16),
            pltpu.VMEM((rows, width), BF16),
            shape_of(*wire),
            *norm_shapes,
        ),
        name="middle",
        compiler_params=PARAMS,
    )(returned, normal_first, std_first, y_second, grad_first, space_qkv, space_out, time_out)
    vmem = pl.BlockSpec(memory_space=pltpu.VMEM)
    time_rows, x_second, dx_first = pl.pallas_call(
        time_kernel,
        out_shape=(
            shape_of(*wire),
            pltpu.HBM((rows, width), BF16),
            pltpu.HBM((rows, width), BF16),
        ),
        out_specs=(vmem, hbm, hbm),
        scratch_shapes=[
            pltpu.VMEM((rows, width + INNER), BF16),
            pltpu.VMEM((rows, 3 * INNER), BF16),
            pltpu.VMEM((HEADS // 2, rows, 4 * rows), F32),
            pltpu.VMEM((HEADS // 2, rows, 4 * rows), BF16),
            pltpu.VMEM((rows, 3 * INNER), BF16),
            pltpu.SemaphoreType.DMA((2,)),
        ],
        name="time_attention",
        compiler_params=PARAMS,
    )(exchange(time_send, "tm"), time_qkv, x_second, dx_first)
    x_first, dx_second = pl.pallas_call(
        last_kernel,
        out_shape=(pltpu.HBM((rows, width), BF16), pltpu.HBM((rows, width), BF16)),
        out_specs=(hbm, hbm),
        scratch_shapes=[
            pltpu.VMEM((rows, width + INNER), BF16),
            pltpu.VMEM((rows, width), BF16),
            pltpu.VMEM((rows, width), BF16),
            pltpu.SemaphoreType.DMA((5,)),
        ],
        name="last",
        compiler_params=PARAMS,
    )(exchange(time_rows, "tm"), y_first, normal_second, std_second, grad_second, time_out)
    return tuple(a.reshape(shape) for a in (x_first, x_second, dx_first, dx_second))


def solution(mesh):
    in_specs = (
        P(None, "tm", "space", None),
        P(None, "tm", "space", None),
        P(None, "tm", "space", None),
        P(None, "tm", "space", None),
        P("tm", None),
        P(),
        P(),
        P(),
        P(),
    )
    out_specs = (
        P(None, "tm", "space", None),
        P(None, "tm", "space", None),
        P(None, "tm", "space", None),
        P(None, "tm", "space", None),
    )
    return jax.shard_map(
        per_device, mesh=mesh, in_specs=in_specs, out_specs=out_specs, check_vma=False
    )
```
